256 devices in a mesh: tile: 4 (over y), proj: 16 (over x, z_hi, core), cuts: 4 (over z_lo).
Axes of the slice: x: 4, y: 4, z: 8 (z_hi: 2, z_lo: 4; z = z_hi * 4 + z_lo), core: 2. Of those that a mesh axis runs over, the one named last changes fastest.
Arguments:
- object_field: float32 [64, 2, 384, 2048], P(('proj', 'cuts'), None, None, 'tile'), may hold values from -5 to 5
- probe_field: float32 [2, 256, 256], replicated, may hold values from -6 to 6
- amplitudes: bfloat16 [64, 4, 6, 256, 256], P(('proj', 'cuts'), 'tile'), may hold values from 0 to 16
- pos_rows: int32 [64, 4, 6], P(('proj', 'cuts'), 'tile'), may hold values from 0 to 128
- pos_cols: int32 [64, 4, 6], P(('proj', 'cuts'), 'tile'), may hold values from 0 to 512
- counts: int32 [64, 4], P(('proj', 'cuts'), 'tile'), may hold values from 1 to 6, as said below
- admm_dual: float32 [64, 32, 2048], P(('proj', 'cuts'), None, 'tile'), may hold values from -4 to 4
- volume: float32 [32, 2048, 2048], P('cuts', ('tile', 'proj')), may hold values from -6 to 6
- proj_weights: bfloat16 [16, 2048, 2048], P(None, ('tile', 'proj')), may hold values from -0.125 to 0.125
- ray_weights: float32 [16, 2048], replicated, may hold values from -0.125 to 0.125
- angle_ids: int32 [64], replicated, may hold values from 0 to 15
Outputs:
- new_object: float32 [64, 2, 384, 2048], P(('proj', 'cuts'), None, None, 'tile')
- new_probe: float32 [2, 256, 256], replicated
- new_volume: float32 [32, 2048, 2048], P('cuts', ('tile', 'proj'))
The draws below stay inside these ranges and needn't reach their ends.
Inputs may be any that keep to these rules, and one draw needn't show every extreme that they name: `counts`: every tile holds at least one live position and at most 6; exactly one tile of one projection holds 6, every other holds at most 3.
All inputs are finite; a program needn't handle non-finite values.
Results may differ from the reference program's by a relative error of at most 0.00095.
The reference program's roundings to bfloat16 on the way count: a program that leaves them out, or rounds other values in their place, can miss the bound.
Values may be sent and summed in bfloat16 or wider, within the bound.
A program may use at most 64 MiB of HBM per device.

```python
import math
import jax
import jax.numpy as jnp
from jax import lax

PB = 256
W = 2048
PR = 384
CAP = 6
SLAB = 32
NANG = 16
A = 64
COLS_DEV = 512
N_TILE = 4


def draw_counts(key, part):
    first_key, second_key = jax.random.split(jax.random.fold_in(key, 17))
    base = jax.random.randint(first_key, (A, N_TILE), 1, CAP // 2 + 1)
    chosen = jax.random.randint(second_key, (), 0, A * N_TILE)
    positions = jnp.arange(A * N_TILE, dtype=jnp.int32).reshape(A, N_TILE)
    return jnp.where(positions == chosen, CAP, base).astype(jnp.int32)


def with_ends(values, own_key, smallest, high):
    shape = values.shape
    place = [jax.random.randint(jax.random.fold_in(own_key, axis), (), 0, shape[axis]) for axis in range(len(shape))]
    values = values.at[tuple(place)].set(smallest)
    longest = shape.index(max(shape))
    place[longest] = (place[longest] + 1) % shape[longest]
    return values.at[tuple(place)].set(high)


def level_of(key, dims, cuts, least, high):
    loudness, own = 1.0, jax.random.fold_in(key, 6)
    for dim, blocks in cuts:
        steps = jnp.exp(jax.random.uniform(jax.random.fold_in(own, dim), (blocks,), jnp.float32, least / len(cuts), high / len(cuts)))
        loudness = loudness * jnp.repeat(steps, dims[dim] // blocks).reshape([-1 if axis == dim else 1 for axis in range(len(dims))])
    return loudness


def noise(own_key, shape, spread, limit, pieces=(), kind=jnp.bfloat16):
    array = jax.random.normal(own_key, shape, jnp.float32) * spread
    if len(pieces) > 0:
        array = level_of(own_key, shape, pieces, -0.22, 0.18) * array
    return jnp.clip(array, min=-limit, max=limit).astype(kind)


def setup_inputs(seed: int = 0) -> dict:
    arg_keys = jax.random.split(jax.random.key(seed), 12)
    object_field = noise(arg_keys[0], (A, 2, PR, W), 0.7, 5.0, ((0, 64), (3, 4)), jnp.float32)
    probe_field = noise(arg_keys[1], (2, PB, PB), 1.0, 6.0, (), jnp.float32)
    amplitudes = jnp.clip(16.0 * jax.random.uniform(arg_keys[2], (A, N_TILE, CAP, PB, PB), jnp.float32) ** level_of(arg_keys[2], (A, N_TILE, CAP, PB, PB), ((0, 64), (1, 4)), -0.2, 0.2), 0.0, 16.0).astype(jnp.bfloat16)
    pos_rows = with_ends(jax.random.randint(arg_keys[3], (A, N_TILE, CAP), 0, PR - PB + 1), jax.random.fold_in(arg_keys[3], 1), 0, PR - PB).astype(jnp.int32)
    pos_cols = with_ends(jax.random.randint(arg_keys[4], (A, N_TILE, CAP), 0, COLS_DEV + 1), jax.random.fold_in(arg_keys[4], 1), 0, COLS_DEV).astype(jnp.int32)
    counts = draw_counts(jax.random.fold_in(arg_keys[11], 71), 0)
    admm_dual = noise(arg_keys[6], (A, SLAB, W), 0.5, 4.0, ((0, 64), (2, 4)), jnp.float32)
    volume = noise(arg_keys[7], (SLAB, W, W), 1.0, 6.0, ((0, 4), (1, 64)), jnp.float32)
    proj_weights = noise(arg_keys[8], (NANG, W, W), W ** -0.5, 0.125, ((1, 64),))
    ray_weights = noise(arg_keys[9], (NANG, W), W ** -0.5, 0.125, (), jnp.float32)
    angle_ids = with_ends(jax.random.randint(arg_keys[10], (A,), 0, NANG), jax.random.fold_in(arg_keys[10], 1), 0, NANG - 1).astype(jnp.int32)
    return {"object_field": object_field, "probe_field": probe_field, "amplitudes": amplitudes, "pos_rows": pos_rows, "pos_cols": pos_cols, "counts": counts, "admm_dual": admm_dual, "volume": volume, "proj_weights": proj_weights, "ray_weights": ray_weights, "angle_ids": angle_ids}


tomo_step = 1.0

def dft_tables(side):
    indices = jnp.arange(side, dtype=jnp.int32)
    products = indices[:, None] * indices[None, :] % side
    phase_angle = products.astype(jnp.float32) * (2.0 * math.pi / side)
    norm_factor = 1.0 / math.sqrt(side)
    return ((jnp.cos(phase_angle) * norm_factor).astype(jnp.bfloat16), (-jnp.sin(phase_angle) * norm_factor).astype(jnp.bfloat16))

def matmul(left, right):
    return jnp.dot(left, right, preferred_element_type=jnp.float32)

def complex_matmul(left_real, left_imag, right_real, right_imag):
    out_real = matmul(left_real, right_real) - matmul(left_imag, right_imag)
    out_imag = matmul(left_real, right_imag) + matmul(left_imag, right_real)
    return (out_real, out_imag)

def patch_terms(patch_real, patch_imag, probe_real, probe_imag, amplitude, dft_real, dft_imag):
    wave_real = (probe_real * patch_real - probe_imag * patch_imag).astype(jnp.bfloat16)
    wave_imag = (probe_real * patch_imag + probe_imag * patch_real).astype(jnp.bfloat16)
    half_real, half_imag = complex_matmul(dft_real, dft_imag, wave_real, wave_imag)
    half_real = half_real.astype(jnp.bfloat16)
    half_imag = half_imag.astype(jnp.bfloat16)
    far_real, far_imag = complex_matmul(half_real, half_imag, dft_real, dft_imag)
    modulus = jnp.sqrt(far_real * far_real + far_imag * far_imag + 0.25)
    factor = amplitude.astype(jnp.float32) / modulus - 1.0
    diff_real = (far_real * factor).astype(jnp.bfloat16)
    diff_imag = (far_imag * factor).astype(jnp.bfloat16)
    conj_imag = -dft_imag
    back_half_real, back_half_imag = complex_matmul(dft_real, conj_imag, diff_real, diff_imag)
    back_half_real = back_half_real.astype(jnp.bfloat16)
    back_half_imag = back_half_imag.astype(jnp.bfloat16)
    back_real, back_imag = complex_matmul(back_half_real, back_half_imag, dft_real, conj_imag)
    object_real = probe_real * back_real + probe_imag * back_imag
    object_imag = probe_real * back_imag - probe_imag * back_real
    probe_grad_real = patch_real * back_real + patch_imag * back_imag
    probe_grad_imag = patch_real * back_imag - patch_imag * back_real
    energy = jnp.mean(patch_real * patch_real + patch_imag * patch_imag)
    return (jnp.stack([object_real, object_imag]), jnp.stack([probe_grad_real, probe_grad_imag]), energy)

def reference(object_field, probe_field, amplitudes, pos_rows, pos_cols, counts, admm_dual, volume, proj_weights, ray_weights, angle_ids):
    half_side = PB // 2
    tile_cols = W // N_TILE
    dft_real, dft_imag = dft_tables(PB)
    probe_real = probe_field[0]
    probe_imag = probe_field[1]
    zero_index = jnp.zeros((), jnp.int32)

    def one_projection(inputs):
        object_one, amp_one, rows_one, cols_one, count_one = inputs
        padded = jnp.pad(object_one, ((0, 0), (0, 0), (half_side, half_side)))
        running = (jnp.zeros(padded.shape, jnp.float32), jnp.zeros((2, PB, PB), jnp.float32), jnp.zeros((), jnp.float32))
        for tile_number in range(N_TILE):

            def slot_step(slot_index, state_tuple):
                grad_sum, probe_sum, energy_sum = state_tuple
                row_at = rows_one[tile_number, slot_index].astype(jnp.int32)
                col_at = (cols_one[tile_number, slot_index] + tile_number * tile_cols).astype(jnp.int32)
                anchor = (zero_index, row_at, col_at)
                object_patch = lax.dynamic_slice(padded, anchor, (2, PB, PB))
                object_part, probe_part, energy = patch_terms(object_patch[0], object_patch[1], probe_real, probe_imag, amp_one[tile_number, slot_index], dft_real, dft_imag)
                current = lax.dynamic_slice(grad_sum, anchor, (2, PB, PB))
                grad_sum = lax.dynamic_update_slice(grad_sum, current + object_part, anchor)
                return (grad_sum, probe_sum + probe_part, energy_sum + energy)
            running = lax.fori_loop(zero_index, count_one[tile_number].astype(jnp.int32), slot_step, running)
        grad_sum, probe_sum, energy_sum = running
        return (grad_sum[:, :, half_side:half_side + W], probe_sum, energy_sum)
    object_grad, probe_parts, energy_parts = lax.map(one_projection, (object_field, amplitudes, pos_rows, pos_cols, counts))
    probe_grad = lax.optimization_barrier(jnp.sum(probe_parts, axis=0))
    energy = jnp.sum(energy_parts)
    new_probe = probe_field + probe_grad / (energy + 1e-05)
    probe_peak = jnp.max(probe_real * probe_real + probe_imag * probe_imag)
    new_object = object_field + object_grad / (probe_peak + 1e-05)
    first_row = (PR - SLAB) // 2
    target = new_object[:, 1, first_row:first_row + SLAB, :] + admm_dual
    ray_table = ray_weights[angle_ids]
    ray_sums = jnp.einsum('zxy,ay->azx', volume, ray_table, precision=lax.Precision.HIGHEST).astype(jnp.bfloat16)

    def one_angle(inputs):
        sums_one, target_one, angle_one = inputs
        weights_one = lax.dynamic_index_in_dim(proj_weights, angle_one.astype(jnp.int32), 0, keepdims=False)
        forward = matmul(sums_one, weights_one)
        residual = (forward - target_one).astype(jnp.bfloat16)
        return lax.dot_general(residual, weights_one, (((1,), (1,)), ((), ())), preferred_element_type=jnp.float32)
    back_sums = lax.map(one_angle, (ray_sums, target, angle_ids))
    gradient = jnp.einsum('azx,ay->zxy', back_sums, ray_table, precision=lax.Precision.HIGHEST)
    new_volume = volume - tomo_step * gradient
    return (new_object, new_probe, new_volume)
```

```python
import math

import jax
import jax.numpy as jnp
from jax import lax
from jax.sharding import PartitionSpec as P

PB = 256


tomo_step = 1.0


def shifted(value, axis, steps):
    count = lax.axis_size(axis)
    leading, last = (max(0, -steps), min(count, count - steps))
    return lax.ppermute(value, axis, [(source, source + steps) for source in range(leading, last)])


def dft_tables(side):
    indices = jnp.arange(side, dtype=jnp.int32)
    products = indices[:, None] * indices[None, :] % side
    phase_angle = products.astype(jnp.float32) * (2.0 * math.pi / side)
    norm_factor = 1.0 / math.sqrt(side)
    return (
        (jnp.cos(phase_angle) * norm_factor).astype(jnp.bfloat16),
        (-jnp.sin(phase_angle) * norm_factor).astype(jnp.bfloat16),
    )


def matmul(left, right):
    return jnp.dot(left, right, preferred_element_type=jnp.float32)


def complex_matmul(left_real, left_imag, right_real, right_imag):
    out_real = matmul(left_real, right_real) - matmul(left_imag, right_imag)
    out_imag = matmul(left_real, right_imag) + matmul(left_imag, right_real)
    return (out_real, out_imag)


def patch_terms(patch_real, patch_imag, probe_real, probe_imag, amplitude, dft_real, dft_imag):
    wave_real = (probe_real * patch_real - probe_imag * patch_imag).astype(jnp.bfloat16)
    wave_imag = (probe_real * patch_imag + probe_imag * patch_real).astype(jnp.bfloat16)
    half_real, half_imag = complex_matmul(dft_real, dft_imag, wave_real, wave_imag)
    half_real = half_real.astype(jnp.bfloat16)
    half_imag = half_imag.astype(jnp.bfloat16)
    far_real, far_imag = complex_matmul(half_real, half_imag, dft_real, dft_imag)
    modulus = jnp.sqrt(far_real * far_real + far_imag * far_imag + 0.25)
    factor = amplitude.astype(jnp.float32) / modulus - 1.0
    diff_real = (far_real * factor).astype(jnp.bfloat16)
    diff_imag = (far_imag * factor).astype(jnp.bfloat16)
    conj_imag = -dft_imag
    back_half_real, back_half_imag = complex_matmul(dft_real, conj_imag, diff_real, diff_imag)
    back_half_real = back_half_real.astype(jnp.bfloat16)
    back_half_imag = back_half_imag.astype(jnp.bfloat16)
    back_real, back_imag = complex_matmul(back_half_real, back_half_imag, dft_real, conj_imag)
    object_real = probe_real * back_real + probe_imag * back_imag
    object_imag = probe_real * back_imag - probe_imag * back_real
    probe_grad_real = patch_real * back_real + patch_imag * back_imag
    probe_grad_imag = patch_real * back_imag - patch_imag * back_real
    energy = jnp.mean(patch_real * patch_real + patch_imag * patch_imag)
    return (
        jnp.stack([object_real, object_imag]),
        jnp.stack([probe_grad_real, probe_grad_imag]),
        energy,
    )


def tile_edges(values, offset):
    return shifted(values, "tile", offset)


def on_device(
    object_field,
    probe_field,
    amplitudes,
    pos_rows,
    pos_cols,
    counts,
    admm_dual,
    volume,
    proj_weights,
    ray_weights,
    angle_ids,
):
    half_side = PB // 2
    own_object = object_field[0]
    tile_cols = own_object.shape[2]
    from_left = tile_edges(own_object[:, :, tile_cols - half_side :], 1)
    from_right = tile_edges(own_object[:, :, :half_side], -1)
    extended = jnp.concatenate([from_left, own_object, from_right], axis=2)
    dft_real, dft_imag = dft_tables(PB)
    probe_real = probe_field[0]
    probe_imag = probe_field[1]
    zero_index = jnp.zeros((), jnp.int32)
    live_count = counts[0, 0]
    slot_total = amplitudes.shape[2]

    def slot_step(slot_index, state_tuple, weight):
        grad_sum, probe_sum, energy_sum = state_tuple
        anchor = (zero_index, pos_rows[0, 0, slot_index], pos_cols[0, 0, slot_index])
        object_patch = lax.dynamic_slice(extended, anchor, (2, PB, PB))
        object_part, probe_part, energy = patch_terms(
            object_patch[0],
            object_patch[1],
            probe_real,
            probe_imag,
            amplitudes[0, 0, slot_index],
            dft_real,
            dft_imag,
        )
        current = lax.dynamic_slice(grad_sum, anchor, (2, PB, PB))
        grad_sum = lax.dynamic_update_slice(grad_sum, current + weight * object_part, anchor)
        return (grad_sum, probe_sum + weight * probe_part, energy_sum + weight * energy)

    running = (
        jnp.zeros(extended.shape, jnp.float32),
        jnp.zeros((2, PB, PB), jnp.float32),
        jnp.zeros((), jnp.float32),
    )
    running = lax.fori_loop(
        0,
        slot_total,
        lambda slot_index, state_tuple: slot_step(
            slot_index, state_tuple, (slot_index < live_count).astype(jnp.float32)
        ),
        running,
    )
    grad_sum, probe_sum, energy_sum = running
    to_right_edge = tile_edges(grad_sum[:, :, :half_side], -1)
    to_left_edge = tile_edges(grad_sum[:, :, tile_cols + half_side :], 1)
    own_cells = grad_sum[:, :, half_side : half_side + tile_cols]
    own_cells = own_cells.at[:, :, :half_side].add(to_left_edge)
    own_cells = own_cells.at[:, :, tile_cols - half_side :].add(to_right_edge)
    probe_flat = jnp.concatenate(
        [probe_sum.reshape(-1), jnp.broadcast_to(energy_sum, (128,))]
    )
    probe_flat = lax.psum(probe_flat, ("tile", "proj", "cuts"))
    probe_grad = probe_flat[: probe_sum.size].reshape(probe_sum.shape)
    energy = probe_flat[probe_sum.size]
    new_probe = probe_field + probe_grad / (energy + 1e-05)
    probe_peak = jnp.max(probe_real * probe_real + probe_imag * probe_imag)
    new_object = (own_object + own_cells / (probe_peak + 1e-05))[None]
    slab_total = admm_dual.shape[1]
    first_row = (own_object.shape[1] - slab_total) // 2
    slab_values = new_object[:, 1, first_row : first_row + slab_total, :] + admm_dual
    arrived = lax.all_to_all(
        lax.all_to_all(slab_values, "proj", split_axis=2, concat_axis=0, tiled=True),
        "cuts",
        split_axis=1,
        concat_axis=0,
        tiled=True,
    )
    proj_count = lax.axis_size("proj")
    cuts_count = lax.axis_size("cuts")
    slab_dev = arrived.shape[1]
    u_share = arrived.shape[2]
    projections = proj_count * cuts_count
    arrived = arrived.reshape(cuts_count, proj_count, slab_dev, u_share).transpose(1, 0, 2, 3)
    target = (
        arrived.reshape(projections, slab_dev, u_share)
        .transpose(2, 0, 1)
        .reshape(u_share, projections * slab_dev)
    )
    angle_count = ray_weights.shape[0]
    x_share = volume.shape[1]
    width = volume.shape[2]
    onehot = (angle_ids[:, None] == jnp.arange(angle_count, dtype=jnp.int32)[None, :]).astype(
        jnp.float32
    )
    ray_table = jnp.dot(
        onehot, ray_weights, precision=lax.Precision.HIGHEST, preferred_element_type=jnp.float32
    )
    ray_sums = jnp.einsum("zxy,ay->azx", volume, ray_table, precision=lax.Precision.HIGHEST).astype(
        jnp.bfloat16
    )
    spread = onehot.astype(jnp.bfloat16)[:, :, None, None] * ray_sums[:, None, :, :]
    spread = spread.transpose(1, 3, 0, 2).reshape(angle_count * x_share, projections * slab_dev)
    weight_flat = proj_weights.reshape(angle_count * x_share, width)
    partial_term = lax.dot_general(
        weight_flat, spread, (((0,), (0,)), ((), ())), preferred_element_type=jnp.float32
    )
    own_rows = lax.psum_scatter(partial_term, ("tile", "proj"), scatter_dimension=0, tiled=True)
    own_residue = (own_rows - target).astype(jnp.bfloat16)
    residue = lax.all_gather(own_residue, ("tile", "proj"), axis=0, tiled=True)
    backproj = matmul(weight_flat, residue)
    backproj = backproj.reshape(angle_count, x_share, projections, slab_dev)
    back_sums = jnp.einsum("gxaz,ag->azx", backproj, onehot, precision=lax.Precision.HIGHEST)
    gradient = jnp.einsum("azx,ay->zxy", back_sums, ray_table, precision=lax.Precision.HIGHEST)
    new_volume = volume - tomo_step * gradient
    return (new_object, new_probe, new_volume)


def solution(mesh):
    in_specs = (
        P(("proj", "cuts"), None, None, "tile"),
        P(),
        P(("proj", "cuts"), "tile", None, None, None),
        P(("proj", "cuts"), "tile", None),
        P(("proj", "cuts"), "tile", None),
        P(("proj", "cuts"), "tile"),
        P(("proj", "cuts"), None, "tile"),
        P("cuts", ("tile", "proj"), None),
        P(None, ("tile", "proj"), None),
        P(),
        P(),
    )
    out_specs = (P(("proj", "cuts"), None, None, "tile"), P(), P("cuts", ("tile", "proj"), None))
    return jax.shard_map(
        on_device, mesh=mesh, in_specs=in_specs, out_specs=out_specs, check_vma=False
    )
```

```python
import math

import jax
import jax.numpy as jnp
from jax import lax
from jax.experimental import pallas as pl
from jax.experimental.pallas import tpu as pltpu
from jax.sharding import PartitionSpec as P

PB = 256


tomo_step = 1.0


def shifted(value, axis, steps):
    count = lax.axis_size(axis)
    leading, last = (max(0, -steps), min(count, count - steps))
    return lax.ppermute(value, axis, [(source, source + steps) for source in range(leading, last)])


def dft_tables(side):
    indices = jnp.arange(side, dtype=jnp.int32)
    products = indices[:, None] * indices[None, :] % side
    phase_angle = products.astype(jnp.float32) * (2.0 * math.pi / side)
    norm_factor = 1.0 / math.sqrt(side)
    return (
        (jnp.cos(phase_angle) * norm_factor).astype(jnp.bfloat16),
        (-jnp.sin(phase_angle) * norm_factor).astype(jnp.bfloat16),
    )


def matmul(left, right):
    return jnp.dot(left, right, preferred_element_type=jnp.float32)


def complex_matmul(left_real, left_imag, right_real, right_imag):
    out_real = matmul(left_real, right_real) - matmul(left_imag, right_imag)
    out_imag = matmul(left_real, right_imag) + matmul(left_imag, right_real)
    return (out_real, out_imag)


def patch_terms(patch_real, patch_imag, probe_real, probe_imag, amplitude, dft_real, dft_imag):
    wave_real = (probe_real * patch_real - probe_imag * patch_imag).astype(jnp.bfloat16)
    wave_imag = (probe_real * patch_imag + probe_imag * patch_real).astype(jnp.bfloat16)
    half_real, half_imag = complex_matmul(dft_real, dft_imag, wave_real, wave_imag)
    half_real = half_real.astype(jnp.bfloat16)
    half_imag = half_imag.astype(jnp.bfloat16)
    far_real, far_imag = complex_matmul(half_real, half_imag, dft_real, dft_imag)
    modulus = jnp.sqrt(far_real * far_real + far_imag * far_imag + 0.25)
    factor = amplitude.astype(jnp.float32) / modulus - 1.0
    diff_real = (far_real * factor).astype(jnp.bfloat16)
    diff_imag = (far_imag * factor).astype(jnp.bfloat16)
    conj_imag = -dft_imag
    back_half_real, back_half_imag = complex_matmul(dft_real, conj_imag, diff_real, diff_imag)
    back_half_real = back_half_real.astype(jnp.bfloat16)
    back_half_imag = back_half_imag.astype(jnp.bfloat16)
    back_real, back_imag = complex_matmul(back_half_real, back_half_imag, dft_real, conj_imag)
    object_real = probe_real * back_real + probe_imag * back_imag
    object_imag = probe_real * back_imag - probe_imag * back_real
    probe_grad_real = patch_real * back_real + patch_imag * back_imag
    probe_grad_imag = patch_real * back_imag - patch_imag * back_real
    energy = jnp.mean(patch_real * patch_real + patch_imag * patch_imag)
    return (
        jnp.stack([object_real, object_imag]),
        jnp.stack([probe_grad_real, probe_grad_imag]),
        energy,
    )


def bit_steps(axes):
    steps = []
    for axis in axes:
        bits = lax.axis_size(axis).bit_length() - 1
        steps += [(axis, bit) for bit in reversed(range(bits))]
    return steps


def exchange(values, axis, bit):
    count = lax.axis_size(axis)
    return lax.ppermute(values, axis, [(source, source ^ (1 << bit)) for source in range(count)])


def halving_scatter(values, steps):
    for axis, bit in steps:
        mine = (lax.axis_index(axis) >> bit) & 1
        half = values.shape[0] // 2
        keep = lax.dynamic_slice_in_dim(values, mine * half, half, 0)
        send = lax.dynamic_slice_in_dim(values, (1 - mine) * half, half, 0)
        values = keep + exchange(send, axis, bit)
    return values


def doubling_gather(values, steps):
    for axis, bit in reversed(steps):
        mine = (lax.axis_index(axis) >> bit) & 1
        other = exchange(values, axis, bit)
        values = jnp.where(
            mine == 0,
            jnp.concatenate([values, other], axis=0),
            jnp.concatenate([other, values], axis=0),
        )
    return values


def stacked_tables(dft_real, dft_imag):
    rows = lambda top, bottom: jnp.concatenate([top, bottom], axis=0)
    cols = lambda left, right: jnp.concatenate([left, right], axis=1)
    return (
        rows(dft_real, dft_imag),
        rows(-dft_imag, dft_real),
        cols(dft_real, dft_imag),
        cols(-dft_imag, dft_real),
        rows(dft_real, -dft_imag),
        rows(dft_imag, dft_real),
        cols(dft_real, -dft_imag),
        cols(dft_imag, dft_real),
    )


def patch_kernel(count_ref, patch_ref, amp_ref, probe_ref, *refs):
    tables = refs[:8]
    object_ref, probe_sum_ref, energy_ref = refs[8:]
    slot = pl.program_id(0)
    side = probe_ref.shape[1]

    @pl.when(slot == 0)
    def _():
        probe_sum_ref[...] = jnp.zeros(probe_sum_ref.shape, jnp.float32)
        energy_ref[...] = jnp.zeros(energy_ref.shape, jnp.float32)

    @pl.when(slot >= count_ref[0])
    def _():
        object_ref[...] = jnp.zeros(object_ref.shape, jnp.float32)

    @pl.when(slot < count_ref[0])
    def _():
        dot = lambda left, right: jnp.dot(left, right, preferred_element_type=jnp.float32)
        left_1a, left_1b, right_2a, right_2b, left_3a, left_3b, right_4a, right_4b = (
            table[...] for table in tables
        )
        patch_real = patch_ref[0, 0]
        patch_imag = patch_ref[0, 1]
        probe_real = probe_ref[0]
        probe_imag = probe_ref[1]
        wave_real = (probe_real * patch_real - probe_imag * patch_imag).astype(jnp.bfloat16)
        wave_imag = (probe_real * patch_imag + probe_imag * patch_real).astype(jnp.bfloat16)
        half = (dot(left_1a, wave_real) + dot(left_1b, wave_imag)).astype(jnp.bfloat16)
        far = dot(half[:side], right_2a) + dot(half[side:], right_2b)
        far_real = far[:, :side]
        far_imag = far[:, side:]
        modulus = jnp.sqrt(far_real * far_real + far_imag * far_imag + 0.25)
        factor = amp_ref[0].astype(jnp.float32) / modulus - 1.0
        diff_real = (far_real * factor).astype(jnp.bfloat16)
        diff_imag = (far_imag * factor).astype(jnp.bfloat16)
        back_half = (dot(left_3a, diff_real) + dot(left_3b, diff_imag)).astype(jnp.bfloat16)
        back = dot(back_half[:side], right_4a) + dot(back_half[side:], right_4b)
        back_real = back[:, :side]
        back_imag = back[:, side:]
        object_ref[0, 0] = probe_real * back_real + probe_imag * back_imag
        object_ref[0, 1] = probe_real * back_imag - probe_imag * back_real
        probe_sum_ref[0] += patch_real * back_real + patch_imag * back_imag
        probe_sum_ref[1] += patch_real * back_imag - patch_imag * back_real
        energy = jnp.sum(patch_real * patch_real + patch_imag * patch_imag) / (side * side)
        energy_ref[...] += energy


def patch_terms_all(count, patches, amps, probe_field, tables):
    slots, _, side, _ = patches.shape
    full = lambda shape: pl.BlockSpec(shape, lambda slot, count_ref: (0,) * len(shape))
    grid_spec = pltpu.PrefetchScalarGridSpec(
        num_scalar_prefetch=1,
        grid=(slots,),
        in_specs=[
            pl.BlockSpec((1, 2, side, side), lambda slot, count_ref: (slot, 0, 0, 0)),
            pl.BlockSpec((1, side, side), lambda slot, count_ref: (slot, 0, 0)),
            full((2, side, side)),
        ]
        + [full(table.shape) for table in tables],
        out_specs=[
            pl.BlockSpec((1, 2, side, side), lambda slot, count_ref: (slot, 0, 0, 0)),
            full((2, side, side)),
            full((8, 128)),
        ],
    )
    return pl.pallas_call(
        patch_kernel,
        grid_spec=grid_spec,
        out_shape=[
            jax.ShapeDtypeStruct(patches.shape, jnp.float32),
            jax.ShapeDtypeStruct((2, side, side), jnp.float32),
            jax.ShapeDtypeStruct((8, 128), jnp.float32),
        ],
        compiler_params=pltpu.CompilerParams(dimension_semantics=("arbitrary",)),
    )(count, patches, amps, probe_field, *tables)


def tile_edges(values, offset):
    return shifted(values, "tile", offset)


def on_device(
    object_field,
    probe_field,
    amplitudes,
    pos_rows,
    pos_cols,
    counts,
    admm_dual,
    volume,
    proj_weights,
    ray_weights,
    angle_ids,
):
    half_side = PB // 2
    own_object = object_field[0]
    tile_cols = own_object.shape[2]
    from_left = tile_edges(own_object[:, :, tile_cols - half_side :], 1)
    from_right = tile_edges(own_object[:, :, :half_side], -1)
    extended = jnp.concatenate([from_left, own_object, from_right], axis=2)
    dft_real, dft_imag = dft_tables(PB)
    probe_real = probe_field[0]
    probe_imag = probe_field[1]
    zero_index = jnp.zeros((), jnp.int32)
    live_count = counts[0, 0]
    slot_total = amplitudes.shape[2]

    anchors = [
        (zero_index, pos_rows[0, 0, slot_index], pos_cols[0, 0, slot_index])
        for slot_index in range(slot_total)
    ]
    patches = jnp.stack([lax.dynamic_slice(extended, anchor, (2, PB, PB)) for anchor in anchors])
    object_parts, probe_sum, energy_rows = patch_terms_all(
        counts[0, :1],
        patches,
        amplitudes[0, 0],
        probe_field,
        stacked_tables(dft_real, dft_imag),
    )
    energy_sum = energy_rows[0, 0]

    def add_part(slot_index, grad_sum):
        anchor = (zero_index, pos_rows[0, 0, slot_index], pos_cols[0, 0, slot_index])
        current = lax.dynamic_slice(grad_sum, anchor, (2, PB, PB))
        return lax.dynamic_update_slice(grad_sum, current + object_parts[slot_index], anchor)

    grad_sum = lax.fori_loop(0, live_count, add_part, jnp.zeros(extended.shape, jnp.float32))
    to_right_edge = tile_edges(grad_sum[:, :, :half_side], -1)
    to_left_edge = tile_edges(grad_sum[:, :, tile_cols + half_side :], 1)
    own_cells = grad_sum[:, :, half_side : half_side + tile_cols]
    own_cells = own_cells.at[:, :, :half_side].add(to_left_edge)
    own_cells = own_cells.at[:, :, tile_cols - half_side :].add(to_right_edge)
    probe_steps = bit_steps(("proj", "tile", "cuts"))
    probe_rows = probe_sum.size // 128
    padded_rows = -(-(probe_rows + 1) // 2 ** len(probe_steps)) * 2 ** len(probe_steps)
    probe_flat = jnp.concatenate(
        [
            probe_sum.reshape(probe_rows, 128),
            jnp.broadcast_to(energy_sum, (1, 128)),
            jnp.zeros((padded_rows - probe_rows - 1, 128), jnp.float32),
        ]
    )
    probe_flat = doubling_gather(halving_scatter(probe_flat, probe_steps), probe_steps)
    probe_grad = probe_flat[:probe_rows].reshape(probe_sum.shape)
    energy = probe_flat[probe_rows, 0]
    new_probe = probe_field + probe_grad / (energy + 1e-05)
    probe_peak = jnp.max(probe_real * probe_real + probe_imag * probe_imag)
    new_object = (own_object + own_cells / (probe_peak + 1e-05))[None]
    slab_total = admm_dual.shape[1]
    first_row = (own_object.shape[1] - slab_total) // 2
    slab_values = new_object[:, 1, first_row : first_row + slab_total, :] + admm_dual
    arrived = lax.all_to_all(
        lax.all_to_all(slab_values, "proj", split_axis=2, concat_axis=0, tiled=True),
        "cuts",
        split_axis=1,
        concat_axis=0,
        tiled=True,
    )
    proj_count = lax.axis_size("proj")
    cuts_count = lax.axis_size("cuts")
    slab_dev = arrived.shape[1]
    u_share = arrived.shape[2]
    projections = proj_count * cuts_count
    arrived = arrived.reshape(cuts_count, proj_count, slab_dev, u_share).transpose(1, 0, 2, 3)
    target = (
        arrived.reshape(projections, slab_dev, u_share)
        .transpose(2, 0, 1)
        .reshape(u_share, projections * slab_dev)
    )
    angle_count = ray_weights.shape[0]
    x_share = volume.shape[1]
    width = volume.shape[2]
    onehot = (angle_ids[:, None] == jnp.arange(angle_count, dtype=jnp.int32)[None, :]).astype(
        jnp.float32
    )
    ray_table = jnp.dot(
        onehot, ray_weights, precision=lax.Precision.HIGHEST, preferred_element_type=jnp.float32
    )
    ray_sums = jnp.einsum("zxy,ay->azx", volume, ray_table, precision=lax.Precision.HIGHEST).astype(
        jnp.bfloat16
    )
    spread = onehot.astype(jnp.bfloat16)[:, :, None, None] * ray_sums[:, None, :, :]
    spread = spread.transpose(1, 3, 0, 2).reshape(angle_count * x_share, projections * slab_dev)
    weight_flat = proj_weights.reshape(angle_count * x_share, width)
    partial_term = lax.dot_general(
        weight_flat, spread, (((0,), (0,)), ((), ())), preferred_element_type=jnp.float32
    )
    volume_steps = bit_steps(("tile", "proj"))
    own_rows = halving_scatter(partial_term, volume_steps)
    own_residue = (own_rows - target).astype(jnp.bfloat16)
    residue = doubling_gather(own_residue, volume_steps)
    backproj = matmul(weight_flat, residue)
    backproj = backproj.reshape(angle_count, x_share, projections, slab_dev)
    back_sums = jnp.einsum("gxaz,ag->azx", backproj, onehot, precision=lax.Precision.HIGHEST)
    gradient = jnp.einsum("azx,ay->zxy", back_sums, ray_table, precision=lax.Precision.HIGHEST)
    new_volume = volume - tomo_step * gradient
    return (new_object, new_probe, new_volume)


def solution(mesh):
    in_specs = (
        P(("proj", "cuts"), None, None, "tile"),
        P(),
        P(("proj", "cuts"), "tile", None, None, None),
        P(("proj", "cuts"), "tile", None),
        P(("proj", "cuts"), "tile", None),
        P(("proj", "cuts"), "tile"),
        P(("proj", "cuts"), None, "tile"),
        P("cuts", ("tile", "proj"), None),
        P(None, ("tile", "proj"), None),
        P(),
        P(),
    )
    out_specs = (P(("proj", "cuts"), None, None, "tile"), P(), P("cuts", ("tile", "proj"), None))
    return jax.shard_map(
        on_device, mesh=mesh, in_specs=in_specs, out_specs=out_specs, check_vma=False
    )
```

```python
import math

import jax
import jax.numpy as jnp
from jax import lax
from jax.experimental import pallas as pl
from jax.experimental.pallas import tpu as pltpu
from jax.sharding import PartitionSpec as P

PB = 256


tomo_step = 1.0


def shifted(value, axis, steps):
    count = lax.axis_size(axis)
    leading, last = (max(0, -steps), min(count, count - steps))
    return lax.ppermute(value, axis, [(source, source + steps) for source in range(leading, last)])


def dft_tables(side):
    indices = jnp.arange(side, dtype=jnp.int32)
    products = indices[:, None] * indices[None, :] % side
    phase_angle = products.astype(jnp.float32) * (2.0 * math.pi / side)
    norm_factor = 1.0 / math.sqrt(side)
    return (
        (jnp.cos(phase_angle) * norm_factor).astype(jnp.bfloat16),
        (-jnp.sin(phase_angle) * norm_factor).astype(jnp.bfloat16),
    )


def matmul(left, right):
    return jnp.dot(left, right, preferred_element_type=jnp.float32)


def complex_matmul(left_real, left_imag, right_real, right_imag):
    out_real = matmul(left_real, right_real) - matmul(left_imag, right_imag)
    out_imag = matmul(left_real, right_imag) + matmul(left_imag, right_real)
    return (out_real, out_imag)


def patch_terms(patch_real, patch_imag, probe_real, probe_imag, amplitude, dft_real, dft_imag):
    wave_real = (probe_real * patch_real - probe_imag * patch_imag).astype(jnp.bfloat16)
    wave_imag = (probe_real * patch_imag + probe_imag * patch_real).astype(jnp.bfloat16)
    half_real, half_imag = complex_matmul(dft_real, dft_imag, wave_real, wave_imag)
    half_real = half_real.astype(jnp.bfloat16)
    half_imag = half_imag.astype(jnp.bfloat16)
    far_real, far_imag = complex_matmul(half_real, half_imag, dft_real, dft_imag)
    modulus = jnp.sqrt(far_real * far_real + far_imag * far_imag + 0.25)
    factor = amplitude.astype(jnp.float32) / modulus - 1.0
    diff_real = (far_real * factor).astype(jnp.bfloat16)
    diff_imag = (far_imag * factor).astype(jnp.bfloat16)
    conj_imag = -dft_imag
    back_half_real, back_half_imag = complex_matmul(dft_real, conj_imag, diff_real, diff_imag)
    back_half_real = back_half_real.astype(jnp.bfloat16)
    back_half_imag = back_half_imag.astype(jnp.bfloat16)
    back_real, back_imag = complex_matmul(back_half_real, back_half_imag, dft_real, conj_imag)
    object_real = probe_real * back_real + probe_imag * back_imag
    object_imag = probe_real * back_imag - probe_imag * back_real
    probe_grad_real = patch_real * back_real + patch_imag * back_imag
    probe_grad_imag = patch_real * back_imag - patch_imag * back_real
    energy = jnp.mean(patch_real * patch_real + patch_imag * patch_imag)
    return (
        jnp.stack([object_real, object_imag]),
        jnp.stack([probe_grad_real, probe_grad_imag]),
        energy,
    )


def axis_bits(axis):
    return lax.axis_size(axis).bit_length() - 1


def bit_steps(axes):
    steps = []
    for axis in axes:
        steps += [(axis, bit) for bit in reversed(range(axis_bits(axis)))]
    return steps


def link_order(steps):
    by_distance = [("proj", 0), ("tile", 0), ("cuts", 0), ("proj", 2), ("tile", 1), ("cuts", 1)]
    ranked = [step for step in by_distance if step in steps]
    return ranked + [step for step in steps if step not in ranked]


def bit_view(values, steps):
    return values.reshape((2,) * len(steps) + (values.shape[0] >> len(steps),) + values.shape[1:])


def ordered_scatter(values, steps, order):
    values = bit_view(values, steps)
    for axis, bit in order:
        place = steps.index((axis, bit))
        mine = (lax.axis_index(axis) >> bit) & 1
        keep = lax.dynamic_slice_in_dim(values, mine, 1, place)
        send = lax.dynamic_slice_in_dim(values, 1 - mine, 1, place)
        values = keep + exchange(send, axis, bit)
    return values.reshape(values.shape[len(steps) :])


def ordered_gather(values, steps, order):
    values = values.reshape((1,) * len(steps) + values.shape)
    for axis, bit in reversed(order):
        place = steps.index((axis, bit))
        mine = (lax.axis_index(axis) >> bit) & 1
        other = exchange(values, axis, bit)
        values = jnp.where(
            mine == 0,
            jnp.concatenate([values, other], axis=place),
            jnp.concatenate([other, values], axis=place),
        )
    return values.reshape((-1,) + values.shape[len(steps) + 1 :])


def exchange(values, axis, bit):
    count = lax.axis_size(axis)
    return lax.ppermute(values, axis, [(source, source ^ (1 << bit)) for source in range(count)])


def halving_scatter(values, steps):
    for axis, bit in steps:
        mine = (lax.axis_index(axis) >> bit) & 1
        half = values.shape[0] // 2
        keep = lax.dynamic_slice_in_dim(values, mine * half, half, 0)
        send = lax.dynamic_slice_in_dim(values, (1 - mine) * half, half, 0)
        values = keep + exchange(send, axis, bit)
    return values


def exchange_sum(values, steps):
    for axis, bit in steps:
        values = values + exchange(values, axis, bit)
    return values


def doubling_gather(values, steps):
    for axis, bit in reversed(steps):
        mine = (lax.axis_index(axis) >> bit) & 1
        other = exchange(values, axis, bit)
        values = jnp.where(
            mine == 0,
            jnp.concatenate([values, other], axis=0),
            jnp.concatenate([other, values], axis=0),
        )
    return values


def stacked_tables(dft_real, dft_imag):
    rows = lambda top, bottom: jnp.concatenate([top, bottom], axis=0)
    cols = lambda left, right: jnp.concatenate([left, right], axis=1)
    return (
        rows(dft_real, dft_imag),
        rows(-dft_imag, dft_real),
        cols(dft_real, dft_imag),
        cols(-dft_imag, dft_real),
        rows(dft_real, -dft_imag),
        rows(dft_imag, dft_real),
        cols(dft_real, -dft_imag),
        cols(dft_imag, dft_real),
    )


def patch_kernel(meta_ref, window_ref, amp_ref, probe_ref, *refs):
    tables = refs[:8]
    grad_ref, probe_sum_ref, energy_ref = refs[8:]
    slot = pl.program_id(0)
    slots = pl.num_programs(0)
    side = probe_ref.shape[1]
    width = window_ref.shape[2]

    @pl.when(slot == 0)
    def _():
        grad_ref[...] = jnp.zeros(grad_ref.shape, jnp.float32)
        probe_sum_ref[...] = jnp.zeros(probe_sum_ref.shape, jnp.float32)
        energy_ref[...] = jnp.zeros(energy_ref.shape, jnp.float32)

    @pl.when(slot < meta_ref[0])
    def _():
        row = meta_ref[1 + slot]
        col = meta_ref[1 + slots + slot]
        band = side + 8
        rows = pl.ds(pl.multiple_of(row // 8 * 8, 8), band)
        row_shift = row % 8
        to_front = (width - col) % width

        def extract(part):
            values = pltpu.roll(window_ref[part, rows, :], (band - row_shift) % band, 0)
            return pltpu.roll(values[:side], to_front, 1)[:, :side]

        patch_real = extract(0)
        patch_imag = extract(1)
        dot = lambda left, right: jnp.dot(left, right, preferred_element_type=jnp.float32)
        left_1a, left_1b, right_2a, right_2b, left_3a, left_3b, right_4a, right_4b = (
            table[...] for table in tables
        )
        probe_real = probe_ref[0]
        probe_imag = probe_ref[1]
        wave_real = (probe_real * patch_real - probe_imag * patch_imag).astype(jnp.bfloat16)
        wave_imag = (probe_real * patch_imag + probe_imag * patch_real).astype(jnp.bfloat16)
        half = (dot(left_1a, wave_real) + dot(left_1b, wave_imag)).astype(jnp.bfloat16)
        far = dot(half[:side], right_2a) + dot(half[side:], right_2b)
        far_real = far[:, :side]
        far_imag = far[:, side:]
        modulus = jnp.sqrt(far_real * far_real + far_imag * far_imag + 0.25)
        factor = amp_ref[0].astype(jnp.float32) / modulus - 1.0
        diff_real = (far_real * factor).astype(jnp.bfloat16)
        diff_imag = (far_imag * factor).astype(jnp.bfloat16)
        back_half = (dot(left_3a, diff_real) + dot(left_3b, diff_imag)).astype(jnp.bfloat16)
        back = dot(back_half[:side], right_4a) + dot(back_half[side:], right_4b)
        back_real = back[:, :side]
        back_imag = back[:, side:]
        filler = jnp.zeros((side, width - side), jnp.float32)
        below = jnp.zeros((8, width), jnp.float32)
        for part, value in enumerate(
            (
                probe_real * back_real + probe_imag * back_imag,
                probe_real * back_imag - probe_imag * back_real,
            )
        ):
            placed = pltpu.roll(jnp.concatenate([value, filler], axis=1), col, 1)
            placed = pltpu.roll(jnp.concatenate([placed, below], axis=0), row_shift, 0)
            grad_ref[part, rows, :] += placed
        probe_sum_ref[0] += patch_real * back_real + patch_imag * back_imag
        probe_sum_ref[1] += patch_real * back_imag - patch_imag * back_real
        energy = jnp.sum(patch_real * patch_real + patch_imag * patch_imag) / (side * side)
        energy_ref[...] += energy


def patch_terms_all(meta, window, amps, probe_field, tables):
    slots, side, _ = amps.shape
    full = lambda shape: pl.BlockSpec(shape, lambda slot, meta_ref: (0,) * len(shape))
    grid_spec = pltpu.PrefetchScalarGridSpec(
        num_scalar_prefetch=1,
        grid=(slots,),
        in_specs=[
            full(window.shape),
            pl.BlockSpec((1, side, side), lambda slot, meta_ref: (slot, 0, 0)),
            full((2, side, side)),
        ]
        + [full(table.shape) for table in tables],
        out_specs=[
            full(window.shape),
            full((2, side, side)),
            full((8, 128)),
        ],
    )
    return pl.pallas_call(
        patch_kernel,
        grid_spec=grid_spec,
        out_shape=[
            jax.ShapeDtypeStruct(window.shape, jnp.float32),
            jax.ShapeDtypeStruct((2, side, side), jnp.float32),
            jax.ShapeDtypeStruct((8, 128), jnp.float32),
        ],
        compiler_params=pltpu.CompilerParams(dimension_semantics=("arbitrary",)),
    )(meta, window, amps, probe_field, *tables)


def tile_edges(values, offset):
    return shifted(values, "tile", offset)


def on_device(
    object_field,
    probe_field,
    amplitudes,
    pos_rows,
    pos_cols,
    counts,
    admm_dual,
    volume,
    proj_weights,
    ray_weights,
    angle_ids,
):
    half_side = PB // 2
    own_object = object_field[0]
    tile_cols = own_object.shape[2]
    from_left = tile_edges(own_object[:, :, tile_cols - half_side :], 1)
    from_right = tile_edges(own_object[:, :, :half_side], -1)
    extended = jnp.concatenate([from_left, own_object, from_right], axis=2)
    dft_real, dft_imag = dft_tables(PB)
    probe_real = probe_field[0]
    probe_imag = probe_field[1]

    spare = -(-extended.shape[2] // 128) * 128 + 128 - extended.shape[2]
    window = jnp.pad(extended, ((0, 0), (0, 8), (0, spare)))
    angle_count = ray_weights.shape[0]
    x_share = volume.shape[1]
    width = volume.shape[2]
    onehot = (angle_ids[:, None] == jnp.arange(angle_count, dtype=jnp.int32)[None, :]).astype(
        jnp.float32
    )
    ray_table = jnp.dot(
        onehot, ray_weights, precision=lax.Precision.HIGHEST, preferred_element_type=jnp.float32
    )
    ray_sums = jnp.einsum("zxy,ay->azx", volume, ray_table, precision=lax.Precision.HIGHEST).astype(
        jnp.bfloat16
    )
    spread = onehot.astype(jnp.bfloat16)[:, :, None, None] * ray_sums[:, None, :, :]
    spread = spread.transpose(1, 3, 0, 2).reshape(
        angle_count * x_share, ray_sums.shape[0] * ray_sums.shape[1]
    )
    weight_flat = proj_weights.reshape(angle_count * x_share, width)
    partial_term = lax.dot_general(
        weight_flat, spread, (((0,), (0,)), ((), ())), preferred_element_type=jnp.float32
    )
    volume_steps = bit_steps(("tile", "proj"))
    volume_order = link_order(volume_steps)
    own_rows = ordered_scatter(partial_term, volume_steps, volume_order)
    own_rows, window = lax.optimization_barrier((own_rows, window))
    meta = jnp.concatenate([counts[0, :1], pos_rows[0, 0], pos_cols[0, 0]])
    grad_sum, probe_sum, energy_rows = patch_terms_all(
        meta,
        window,
        amplitudes[0, 0],
        probe_field,
        stacked_tables(dft_real, dft_imag),
    )
    energy_sum = energy_rows[0, 0]
    grad_sum = grad_sum[:, : extended.shape[1]]
    to_right_edge = tile_edges(grad_sum[:, :, :half_side], -1)
    to_left_edge = tile_edges(grad_sum[:, :, tile_cols + half_side : tile_cols + PB], 1)
    own_cells = grad_sum[:, :, half_side : half_side + tile_cols]
    own_cells = own_cells.at[:, :, :half_side].add(to_left_edge)
    own_cells = own_cells.at[:, :, tile_cols - half_side :].add(to_right_edge)
    probe_order = link_order(bit_steps(("proj", "tile", "cuts")))
    probe_steps, probe_rest = probe_order[:3], probe_order[3:]
    probe_rows = probe_sum.size // 128
    padded_rows = -(-(probe_rows + 1) // 2 ** len(probe_steps)) * 2 ** len(probe_steps)
    probe_flat = jnp.concatenate(
        [
            probe_sum.reshape(probe_rows, 128),
            jnp.broadcast_to(energy_sum, (1, 128)),
            jnp.zeros((padded_rows - probe_rows - 1, 128), jnp.float32),
        ]
    )
    probe_flat = exchange_sum(halving_scatter(probe_flat, probe_steps), probe_rest)
    probe_flat = doubling_gather(probe_flat, probe_steps)
    probe_grad = probe_flat[:probe_rows].reshape(probe_sum.shape)
    energy = probe_flat[probe_rows, 0]
    new_probe = probe_field + probe_grad / (energy + 1e-05)
    probe_peak = jnp.max(probe_real * probe_real + probe_imag * probe_imag)
    new_object = (own_object + own_cells / (probe_peak + 1e-05))[None]
    slab_total = admm_dual.shape[1]
    first_row = (own_object.shape[1] - slab_total) // 2
    slab_values = new_object[:, 1, first_row : first_row + slab_total, :] + admm_dual
    arrived = lax.all_to_all(
        lax.all_to_all(slab_values, "proj", split_axis=2, concat_axis=0, tiled=True),
        "cuts",
        split_axis=1,
        concat_axis=0,
        tiled=True,
    )
    proj_count = lax.axis_size("proj")
    cuts_count = lax.axis_size("cuts")
    slab_dev = arrived.shape[1]
    u_share = arrived.shape[2]
    projections = proj_count * cuts_count
    arrived = arrived.reshape(cuts_count, proj_count, slab_dev, u_share).transpose(1, 0, 2, 3)
    target = (
        arrived.reshape(projections, slab_dev, u_share)
        .transpose(2, 0, 1)
        .reshape(u_share, projections * slab_dev)
    )
    own_residue = (own_rows - target).astype(jnp.bfloat16)
    residue = ordered_gather(own_residue, volume_steps, volume_order)
    backproj = matmul(weight_flat, residue)
    backproj = backproj.reshape(angle_count, x_share, projections, slab_dev)
    back_sums = jnp.einsum("gxaz,ag->azx", backproj, onehot, precision=lax.Precision.HIGHEST)
    gradient = jnp.einsum("azx,ay->zxy", back_sums, ray_table, precision=lax.Precision.HIGHEST)
    new_volume = volume - tomo_step * gradient
    return (new_object, new_probe, new_volume)


def solution(mesh):
    in_specs = (
        P(("proj", "cuts"), None, None, "tile"),
        P(),
        P(("proj", "cuts"), "tile", None, None, None),
        P(("proj", "cuts"), "tile", None),
        P(("proj", "cuts"), "tile", None),
        P(("proj", "cuts"), "tile"),
        P(("proj", "cuts"), None, "tile"),
        P("cuts", ("tile", "proj"), None),
        P(None, ("tile", "proj"), None),
        P(),
        P(),
    )
    out_specs = (P(("proj", "cuts"), None, None, "tile"), P(), P("cuts", ("tile", "proj"), None))
    return jax.shard_map(
        on_device, mesh=mesh, in_specs=in_specs, out_specs=out_specs, check_vma=False
    )
```

```python
import math

import jax
import jax.numpy as jnp
from jax import lax
from jax.experimental import pallas as pl
from jax.experimental.pallas import tpu as pltpu
from jax.sharding import PartitionSpec as P

PB = 256


tomo_step = 1.0


def shifted(value, axis, steps):
    count = lax.axis_size(axis)
    leading, last = (max(0, -steps), min(count, count - steps))
    return lax.ppermute(value, axis, [(source, source + steps) for source in range(leading, last)])


def dft_tables(side):
    indices = jnp.arange(side, dtype=jnp.int32)
    products = indices[:, None] * indices[None, :] % side
    phase_angle = products.astype(jnp.float32) * (2.0 * math.pi / side)
    norm_factor = 1.0 / math.sqrt(side)
    return (
        (jnp.cos(phase_angle) * norm_factor).astype(jnp.bfloat16),
        (-jnp.sin(phase_angle) * norm_factor).astype(jnp.bfloat16),
    )


def matmul(left, right):
    return jnp.dot(left, right, preferred_element_type=jnp.float32)


def complex_matmul(left_real, left_imag, right_real, right_imag):
    out_real = matmul(left_real, right_real) - matmul(left_imag, right_imag)
    out_imag = matmul(left_real, right_imag) + matmul(left_imag, right_real)
    return (out_real, out_imag)


def patch_terms(patch_real, patch_imag, probe_real, probe_imag, amplitude, dft_real, dft_imag):
    wave_real = (probe_real * patch_real - probe_imag * patch_imag).astype(jnp.bfloat16)
    wave_imag = (probe_real * patch_imag + probe_imag * patch_real).astype(jnp.bfloat16)
    half_real, half_imag = complex_matmul(dft_real, dft_imag, wave_real, wave_imag)
    half_real = half_real.astype(jnp.bfloat16)
    half_imag = half_imag.astype(jnp.bfloat16)
    far_real, far_imag = complex_matmul(half_real, half_imag, dft_real, dft_imag)
    modulus = jnp.sqrt(far_real * far_real + far_imag * far_imag + 0.25)
    factor = amplitude.astype(jnp.float32) / modulus - 1.0
    diff_real = (far_real * factor).astype(jnp.bfloat16)
    diff_imag = (far_imag * factor).astype(jnp.bfloat16)
    conj_imag = -dft_imag
    back_half_real, back_half_imag = complex_matmul(dft_real, conj_imag, diff_real, diff_imag)
    back_half_real = back_half_real.astype(jnp.bfloat16)
    back_half_imag = back_half_imag.astype(jnp.bfloat16)
    back_real, back_imag = complex_matmul(back_half_real, back_half_imag, dft_real, conj_imag)
    object_real = probe_real * back_real + probe_imag * back_imag
    object_imag = probe_real * back_imag - probe_imag * back_real
    probe_grad_real = patch_real * back_real + patch_imag * back_imag
    probe_grad_imag = patch_real * back_imag - patch_imag * back_real
    energy = jnp.mean(patch_real * patch_real + patch_imag * patch_imag)
    return (
        jnp.stack([object_real, object_imag]),
        jnp.stack([probe_grad_real, probe_grad_imag]),
        energy,
    )


def axis_bits(axis):
    return lax.axis_size(axis).bit_length() - 1


def bit_steps(axes):
    steps = []
    for axis in axes:
        steps += [(axis, bit) for bit in reversed(range(axis_bits(axis)))]
    return steps


def link_order(steps):
    by_distance = [("proj", 0), ("tile", 0), ("cuts", 0), ("proj", 2), ("tile", 1), ("cuts", 1)]
    ranked = [step for step in by_distance if step in steps]
    return ranked + [step for step in steps if step not in ranked]


def cross_order(steps):
    by_distance = [("proj", 0), ("cuts", 0), ("proj", 2), ("tile", 0), ("cuts", 1), ("proj", 3), ("tile", 1)]
    ranked = [step for step in by_distance if step in steps]
    return ranked + [step for step in steps if step not in ranked]


def bit_view(values, steps):
    return values.reshape((2,) * len(steps) + (values.shape[0] >> len(steps),) + values.shape[1:])


def ordered_scatter(values, steps, order):
    values = bit_view(values, steps)
    for axis, bit in order:
        place = steps.index((axis, bit))
        mine = (lax.axis_index(axis) >> bit) & 1
        keep = lax.dynamic_slice_in_dim(values, mine, 1, place)
        send = lax.dynamic_slice_in_dim(values, 1 - mine, 1, place)
        values = keep + exchange(send, axis, bit)
    return values.reshape(values.shape[len(steps) :])


def ordered_gather(values, steps, order):
    values = values.reshape((1,) * len(steps) + values.shape)
    for axis, bit in reversed(order):
        place = steps.index((axis, bit))
        mine = (lax.axis_index(axis) >> bit) & 1
        other = exchange(values, axis, bit)
        values = jnp.where(
            mine == 0,
            jnp.concatenate([values, other], axis=place),
            jnp.concatenate([other, values], axis=place),
        )
    return values.reshape((-1,) + values.shape[len(steps) + 1 :])


def exchange(values, axis, bit):
    count = lax.axis_size(axis)
    return lax.ppermute(values, axis, [(source, source ^ (1 << bit)) for source in range(count)])


def halving_scatter(values, steps):
    for axis, bit in steps:
        mine = (lax.axis_index(axis) >> bit) & 1
        half = values.shape[0] // 2
        keep = lax.dynamic_slice_in_dim(values, mine * half, half, 0)
        send = lax.dynamic_slice_in_dim(values, (1 - mine) * half, half, 0)
        values = keep + exchange(send, axis, bit)
    return values


def doubling_gather(values, steps):
    for axis, bit in reversed(steps):
        mine = (lax.axis_index(axis) >> bit) & 1
        other = exchange(values, axis, bit)
        values = jnp.where(
            mine == 0,
            jnp.concatenate([values, other], axis=0),
            jnp.concatenate([other, values], axis=0),
        )
    return values


def stacked_tables(dft_real, dft_imag):
    rows = lambda top, bottom: jnp.concatenate([top, bottom], axis=0)
    cols = lambda left, right: jnp.concatenate([left, right], axis=1)
    return (
        rows(dft_real, dft_imag),
        rows(-dft_imag, dft_real),
        cols(dft_real, dft_imag),
        cols(-dft_imag, dft_real),
        rows(dft_real, -dft_imag),
        rows(dft_imag, dft_real),
        cols(dft_real, -dft_imag),
        cols(dft_imag, dft_real),
    )


def patch_kernel(meta_ref, window_ref, amp_ref, probe_ref, *refs):
    tables = refs[:8]
    grad_ref, probe_sum_ref, energy_ref = refs[8:]
    slot = pl.program_id(0)
    slots = pl.num_programs(0)
    side = probe_ref.shape[1]
    width = window_ref.shape[2]

    @pl.when(slot == 0)
    def _():
        grad_ref[...] = jnp.zeros(grad_ref.shape, jnp.float32)
        probe_sum_ref[...] = jnp.zeros(probe_sum_ref.shape, jnp.float32)
        energy_ref[...] = jnp.zeros(energy_ref.shape, jnp.float32)

    @pl.when(slot < meta_ref[0])
    def _():
        row = meta_ref[1 + slot]
        col = meta_ref[1 + slots + slot]
        band = side + 8
        rows = pl.ds(pl.multiple_of(row // 8 * 8, 8), band)
        row_shift = row % 8
        to_front = (width - col) % width

        def extract(part):
            values = pltpu.roll(window_ref[part, rows, :], (band - row_shift) % band, 0)
            return pltpu.roll(values[:side], to_front, 1)[:, :side]

        patch_real = extract(0)
        patch_imag = extract(1)
        dot = lambda left, right: jnp.dot(left, right, preferred_element_type=jnp.float32)
        left_1a, left_1b, right_2a, right_2b, left_3a, left_3b, right_4a, right_4b = (
            table[...] for table in tables
        )
        probe_real = probe_ref[0]
        probe_imag = probe_ref[1]
        wave_real = (probe_real * patch_real - probe_imag * patch_imag).astype(jnp.bfloat16)
        wave_imag = (probe_real * patch_imag + probe_imag * patch_real).astype(jnp.bfloat16)
        half = (dot(left_1a, wave_real) + dot(left_1b, wave_imag)).astype(jnp.bfloat16)
        far = dot(half[:side], right_2a) + dot(half[side:], right_2b)
        far_real = far[:, :side]
        far_imag = far[:, side:]
        modulus = jnp.sqrt(far_real * far_real + far_imag * far_imag + 0.25)
        factor = amp_ref[0].astype(jnp.float32) / modulus - 1.0
        diff_real = (far_real * factor).astype(jnp.bfloat16)
        diff_imag = (far_imag * factor).astype(jnp.bfloat16)
        back_half = (dot(left_3a, diff_real) + dot(left_3b, diff_imag)).astype(jnp.bfloat16)
        back = dot(back_half[:side], right_4a) + dot(back_half[side:], right_4b)
        back_real = back[:, :side]
        back_imag = back[:, side:]
        filler = jnp.zeros((side, width - side), jnp.float32)
        below = jnp.zeros((8, width), jnp.float32)
        for part, value in enumerate(
            (
                probe_real * back_real + probe_imag * back_imag,
                probe_real * back_imag - probe_imag * back_real,
            )
        ):
            placed = pltpu.roll(jnp.concatenate([value, filler], axis=1), col, 1)
            placed = pltpu.roll(jnp.concatenate([placed, below], axis=0), row_shift, 0)
            grad_ref[part, rows, :] += placed
        probe_sum_ref[0] += patch_real * back_real + patch_imag * back_imag
        probe_sum_ref[1] += patch_real * back_imag - patch_imag * back_real
        energy = jnp.sum(patch_real * patch_real + patch_imag * patch_imag) / (side * side)
        energy_ref[...] += energy


def patch_terms_all(meta, window, amps, probe_field, tables):
    slots, side, _ = amps.shape
    full = lambda shape: pl.BlockSpec(shape, lambda slot, meta_ref: (0,) * len(shape))
    grid_spec = pltpu.PrefetchScalarGridSpec(
        num_scalar_prefetch=1,
        grid=(slots,),
        in_specs=[
            full(window.shape),
            pl.BlockSpec((1, side, side), lambda slot, meta_ref: (slot, 0, 0)),
            full((2, side, side)),
        ]
        + [full(table.shape) for table in tables],
        out_specs=[
            full(window.shape),
            full((2, side, side)),
            full((8, 128)),
        ],
    )
    return pl.pallas_call(
        patch_kernel,
        grid_spec=grid_spec,
        out_shape=[
            jax.ShapeDtypeStruct(window.shape, jnp.float32),
            jax.ShapeDtypeStruct((2, side, side), jnp.float32),
            jax.ShapeDtypeStruct((8, 128), jnp.float32),
        ],
        compiler_params=pltpu.CompilerParams(dimension_semantics=("arbitrary",)),
    )(meta, window, amps, probe_field, *tables)


def tile_edges(values, offset):
    return shifted(values, "tile", offset)


def on_device(
    object_field,
    probe_field,
    amplitudes,
    pos_rows,
    pos_cols,
    counts,
    admm_dual,
    volume,
    proj_weights,
    ray_weights,
    angle_ids,
):
    half_side = PB // 2
    own_object = object_field[0]
    tile_cols = own_object.shape[2]
    from_left = tile_edges(own_object[:, :, tile_cols - half_side :], 1)
    from_right = tile_edges(own_object[:, :, :half_side], -1)
    extended = jnp.concatenate([from_left, own_object, from_right], axis=2)
    dft_real, dft_imag = dft_tables(PB)
    probe_real = probe_field[0]
    probe_imag = probe_field[1]

    spare = -(-extended.shape[2] // 128) * 128 + 128 - extended.shape[2]
    window = jnp.pad(extended, ((0, 0), (0, 8), (0, spare)))
    meta = jnp.concatenate([counts[0, :1], pos_rows[0, 0], pos_cols[0, 0]])
    grad_sum, probe_sum, energy_rows = patch_terms_all(
        meta,
        window,
        amplitudes[0, 0],
        probe_field,
        stacked_tables(dft_real, dft_imag),
    )
    energy_sum = energy_rows[0, 0]
    grad_sum = grad_sum[:, : extended.shape[1]]
    to_right_edge = tile_edges(grad_sum[:, :, :half_side], -1)
    to_left_edge = tile_edges(grad_sum[:, :, tile_cols + half_side : tile_cols + PB], 1)
    own_cells = grad_sum[:, :, half_side : half_side + tile_cols]
    own_cells = own_cells.at[:, :, :half_side].add(to_left_edge)
    own_cells = own_cells.at[:, :, tile_cols - half_side :].add(to_right_edge)
    probe_bits = bit_steps(("proj", "tile", "cuts"))
    probe_orders = (link_order(probe_bits), cross_order(probe_bits))
    probe_rows = probe_sum.size // 128
    block_rows = 2 ** (len(probe_bits) + 1)
    padded_rows = -(-(probe_rows + 1) // block_rows) * block_rows
    probe_flat = jnp.concatenate(
        [
            probe_sum.reshape(probe_rows, 128),
            jnp.broadcast_to(energy_sum, (1, 128)),
            jnp.zeros((padded_rows - probe_rows - 1, 128), jnp.float32),
        ]
    )
    half_rows = padded_rows // 2
    probe_flat = jnp.concatenate(
        [
            doubling_gather(halving_scatter(probe_flat[start : start + half_rows], order), order)
            for start, order in zip((0, half_rows), probe_orders)
        ]
    )
    probe_grad = probe_flat[:probe_rows].reshape(probe_sum.shape)
    energy = probe_flat[probe_rows, 0]
    new_probe = probe_field + probe_grad / (energy + 1e-05)
    probe_peak = jnp.max(probe_real * probe_real + probe_imag * probe_imag)
    new_object = (own_object + own_cells / (probe_peak + 1e-05))[None]
    slab_total = admm_dual.shape[1]
    first_row = (own_object.shape[1] - slab_total) // 2
    slab_values = new_object[:, 1, first_row : first_row + slab_total, :] + admm_dual
    arrived = lax.all_to_all(
        lax.all_to_all(slab_values, "proj", split_axis=2, concat_axis=0, tiled=True),
        "cuts",
        split_axis=1,
        concat_axis=0,
        tiled=True,
    )
    proj_count = lax.axis_size("proj")
    cuts_count = lax.axis_size("cuts")
    slab_dev = arrived.shape[1]
    u_share = arrived.shape[2]
    projections = proj_count * cuts_count
    arrived = arrived.reshape(cuts_count, proj_count, slab_dev, u_share).transpose(1, 0, 2, 3)
    target = (
        arrived.reshape(projections, slab_dev, u_share)
        .transpose(2, 0, 1)
        .reshape(u_share, projections * slab_dev)
    )
    angle_count = ray_weights.shape[0]
    x_share = volume.shape[1]
    width = volume.shape[2]
    onehot = (angle_ids[:, None] == jnp.arange(angle_count, dtype=jnp.int32)[None, :]).astype(
        jnp.float32
    )
    ray_table = jnp.dot(
        onehot, ray_weights, precision=lax.Precision.HIGHEST, preferred_element_type=jnp.float32
    )
    ray_sums = jnp.einsum("zxy,ay->azx", volume, ray_table, precision=lax.Precision.HIGHEST).astype(
        jnp.bfloat16
    )
    spread = onehot.astype(jnp.bfloat16)[:, :, None, None] * ray_sums[:, None, :, :]
    spread = spread.transpose(1, 3, 0, 2).reshape(angle_count * x_share, projections * slab_dev)
    weight_flat = proj_weights.reshape(angle_count * x_share, width)
    partial_term = lax.dot_general(
        weight_flat, spread, (((0,), (0,)), ((), ())), preferred_element_type=jnp.float32
    )
    volume_steps = bit_steps(("tile", "proj"))
    volume_orders = (link_order(volume_steps), cross_order(volume_steps))
    half_cols = partial_term.shape[1] // 2
    own_rows = jnp.concatenate(
        [
            ordered_scatter(partial_term[:, start : start + half_cols], volume_steps, order)
            for start, order in zip((0, half_cols), volume_orders)
        ],
        axis=1,
    )
    own_residue = (own_rows - target).astype(jnp.bfloat16)
    residue = jnp.concatenate(
        [
            ordered_gather(own_residue[:, start : start + half_cols], volume_steps, order)
            for start, order in zip((0, half_cols), volume_orders)
        ],
        axis=1,
    )
    backproj = matmul(weight_flat, residue)
    backproj = backproj.reshape(angle_count, x_share, projections, slab_dev)
    back_sums = jnp.einsum("gxaz,ag->azx", backproj, onehot, precision=lax.Precision.HIGHEST)
    gradient = jnp.einsum("azx,ay->zxy", back_sums, ray_table, precision=lax.Precision.HIGHEST)
    new_volume = volume - tomo_step * gradient
    return (new_object, new_probe, new_volume)


def solution(mesh):
    in_specs = (
        P(("proj", "cuts"), None, None, "tile"),
        P(),
        P(("proj", "cuts"), "tile", None, None, None),
        P(("proj", "cuts"), "tile", None),
        P(("proj", "cuts"), "tile", None),
        P(("proj", "cuts"), "tile"),
        P(("proj", "cuts"), None, "tile"),
        P("cuts", ("tile", "proj"), None),
        P(None, ("tile", "proj"), None),
        P(),
        P(),
    )
    out_specs = (P(("proj", "cuts"), None, None, "tile"), P(), P("cuts", ("tile", "proj"), None))
    return jax.shard_map(
        on_device, mesh=mesh, in_specs=in_specs, out_specs=out_specs, check_vma=False
    )
```

```python
import math

import jax
import jax.numpy as jnp
from jax import lax
from jax.experimental import pallas as pl
from jax.experimental.pallas import tpu as pltpu
from jax.sharding import PartitionSpec as P

PB = 256


tomo_step = 1.0


def shifted(value, axis, steps):
    count = lax.axis_size(axis)
    leading, last = (max(0, -steps), min(count, count - steps))
    return lax.ppermute(value, axis, [(source, source + steps) for source in range(leading, last)])


def dft_tables(side):
    indices = jnp.arange(side, dtype=jnp.int32)
    products = indices[:, None] * indices[None, :] % side
    phase_angle = products.astype(jnp.float32) * (2.0 * math.pi / side)
    norm_factor = 1.0 / math.sqrt(side)
    return (
        (jnp.cos(phase_angle) * norm_factor).astype(jnp.bfloat16),
        (-jnp.sin(phase_angle) * norm_factor).astype(jnp.bfloat16),
    )


def matmul(left, right):
    return jnp.dot(left, right, preferred_element_type=jnp.float32)


def complex_matmul(left_real, left_imag, right_real, right_imag):
    out_real = matmul(left_real, right_real) - matmul(left_imag, right_imag)
    out_imag = matmul(left_real, right_imag) + matmul(left_imag, right_real)
    return (out_real, out_imag)


def patch_terms(patch_real, patch_imag, probe_real, probe_imag, amplitude, dft_real, dft_imag):
    wave_real = (probe_real * patch_real - probe_imag * patch_imag).astype(jnp.bfloat16)
    wave_imag = (probe_real * patch_imag + probe_imag * patch_real).astype(jnp.bfloat16)
    half_real, half_imag = complex_matmul(dft_real, dft_imag, wave_real, wave_imag)
    half_real = half_real.astype(jnp.bfloat16)
    half_imag = half_imag.astype(jnp.bfloat16)
    far_real, far_imag = complex_matmul(half_real, half_imag, dft_real, dft_imag)
    modulus = jnp.sqrt(far_real * far_real + far_imag * far_imag + 0.25)
    factor = amplitude.astype(jnp.float32) / modulus - 1.0
    diff_real = (far_real * factor).astype(jnp.bfloat16)
    diff_imag = (far_imag * factor).astype(jnp.bfloat16)
    conj_imag = -dft_imag
    back_half_real, back_half_imag = complex_matmul(dft_real, conj_imag, diff_real, diff_imag)
    back_half_real = back_half_real.astype(jnp.bfloat16)
    back_half_imag = back_half_imag.astype(jnp.bfloat16)
    back_real, back_imag = complex_matmul(back_half_real, back_half_imag, dft_real, conj_imag)
    object_real = probe_real * back_real + probe_imag * back_imag
    object_imag = probe_real * back_imag - probe_imag * back_real
    probe_grad_real = patch_real * back_real + patch_imag * back_imag
    probe_grad_imag = patch_real * back_imag - patch_imag * back_real
    energy = jnp.mean(patch_real * patch_real + patch_imag * patch_imag)
    return (
        jnp.stack([object_real, object_imag]),
        jnp.stack([probe_grad_real, probe_grad_imag]),
        energy,
    )


def axis_bits(axis):
    return lax.axis_size(axis).bit_length() - 1


def bit_steps(axes):
    steps = []
    for axis in axes:
        steps += [(axis, bit) for bit in reversed(range(axis_bits(axis)))]
    return steps


def link_order(steps):
    by_distance = [("proj", 0), ("tile", 0), ("cuts", 0), ("proj", 2), ("tile", 1), ("cuts", 1)]
    ranked = [step for step in by_distance if step in steps]
    return ranked + [step for step in steps if step not in ranked]


def bit_view(values, steps):
    return values.reshape((2,) * len(steps) + (values.shape[0] >> len(steps),) + values.shape[1:])


def ordered_scatter(values, steps, order):
    values = bit_view(values, steps)
    for axis, bit in order:
        place = steps.index((axis, bit))
        mine = (lax.axis_index(axis) >> bit) & 1
        keep = lax.dynamic_slice_in_dim(values, mine, 1, place)
        send = lax.dynamic_slice_in_dim(values, 1 - mine, 1, place)
        values = keep + exchange(send, axis, bit)
    return values.reshape(values.shape[len(steps) :])


def ordered_gather(values, steps, order):
    values = values.reshape((1,) * len(steps) + values.shape)
    for axis, bit in reversed(order):
        place = steps.index((axis, bit))
        mine = (lax.axis_index(axis) >> bit) & 1
        other = exchange(values, axis, bit)
        values = jnp.where(
            mine == 0,
            jnp.concatenate([values, other], axis=place),
            jnp.concatenate([other, values], axis=place),
        )
    return values.reshape((-1,) + values.shape[len(steps) + 1 :])


def exchange(values, axis, bit):
    count = lax.axis_size(axis)
    return lax.ppermute(values, axis, [(source, source ^ (1 << bit)) for source in range(count)])


def halving_step(values, axis, bit):
    mine = (lax.axis_index(axis) >> bit) & 1
    half = values.shape[0] // 2
    keep = lax.dynamic_slice_in_dim(values, mine * half, half, 0)
    send = lax.dynamic_slice_in_dim(values, (1 - mine) * half, half, 0)
    return keep + exchange(send, axis, bit)


def doubling_step(values, axis, bit, place=0):
    mine = (lax.axis_index(axis) >> bit) & 1
    other = exchange(values, axis, bit)
    return jnp.where(
        mine == 0,
        jnp.concatenate([values, other], axis=place),
        jnp.concatenate([other, values], axis=place),
    )


def probe_ops(first, rest):
    return (
        [lambda values, step=step: halving_step(values, *step) for step in first]
        + [lambda values, step=step: values + exchange(values, *step) for step in rest]
        + [lambda values, step=step: doubling_step(values, *step) for step in reversed(first)]
    )


def halving_scatter(values, steps):
    for axis, bit in steps:
        mine = (lax.axis_index(axis) >> bit) & 1
        half = values.shape[0] // 2
        keep = lax.dynamic_slice_in_dim(values, mine * half, half, 0)
        send = lax.dynamic_slice_in_dim(values, (1 - mine) * half, half, 0)
        values = keep + exchange(send, axis, bit)
    return values


def exchange_sum(values, steps):
    for axis, bit in steps:
        values = values + exchange(values, axis, bit)
    return values


def doubling_gather(values, steps):
    for axis, bit in reversed(steps):
        mine = (lax.axis_index(axis) >> bit) & 1
        other = exchange(values, axis, bit)
        values = jnp.where(
            mine == 0,
            jnp.concatenate([values, other], axis=0),
            jnp.concatenate([other, values], axis=0),
        )
    return values


def stacked_tables(dft_real, dft_imag):
    rows = lambda top, bottom: jnp.concatenate([top, bottom], axis=0)
    cols = lambda left, right: jnp.concatenate([left, right], axis=1)
    return (
        rows(dft_real, dft_imag),
        rows(-dft_imag, dft_real),
        cols(dft_real, dft_imag),
        cols(-dft_imag, dft_real),
        rows(dft_real, -dft_imag),
        rows(dft_imag, dft_real),
        cols(dft_real, -dft_imag),
        cols(dft_imag, dft_real),
    )


def patch_kernel(meta_ref, window_ref, amp_ref, probe_ref, *refs):
    tables = refs[:8]
    grad_ref, probe_sum_ref, energy_ref = refs[8:]
    slot = pl.program_id(0)
    slots = pl.num_programs(0)
    side = probe_ref.shape[1]
    width = window_ref.shape[2]

    @pl.when(slot == 0)
    def _():
        grad_ref[...] = jnp.zeros(grad_ref.shape, jnp.float32)
        probe_sum_ref[...] = jnp.zeros(probe_sum_ref.shape, jnp.float32)
        energy_ref[...] = jnp.zeros(energy_ref.shape, jnp.float32)

    @pl.when(slot < meta_ref[0])
    def _():
        row = meta_ref[1 + slot]
        col = meta_ref[1 + slots + slot]
        band = side + 8
        rows = pl.ds(pl.multiple_of(row // 8 * 8, 8), band)
        row_shift = row % 8
        to_front = (width - col) % width

        def extract(part):
            values = pltpu.roll(window_ref[part, rows, :], (band - row_shift) % band, 0)
            return pltpu.roll(values[:side], to_front, 1)[:, :side]

        patch_real = extract(0)
        patch_imag = extract(1)
        dot = lambda left, right: jnp.dot(left, right, preferred_element_type=jnp.float32)
        left_1a, left_1b, right_2a, right_2b, left_3a, left_3b, right_4a, right_4b = (
            table[...] for table in tables
        )
        probe_real = probe_ref[0]
        probe_imag = probe_ref[1]
        wave_real = (probe_real * patch_real - probe_imag * patch_imag).astype(jnp.bfloat16)
        wave_imag = (probe_real * patch_imag + probe_imag * patch_real).astype(jnp.bfloat16)
        half = (dot(left_1a, wave_real) + dot(left_1b, wave_imag)).astype(jnp.bfloat16)
        far = dot(half[:side], right_2a) + dot(half[side:], right_2b)
        far_real = far[:, :side]
        far_imag = far[:, side:]
        modulus = jnp.sqrt(far_real * far_real + far_imag * far_imag + 0.25)
        factor = amp_ref[0].astype(jnp.float32) / modulus - 1.0
        diff_real = (far_real * factor).astype(jnp.bfloat16)
        diff_imag = (far_imag * factor).astype(jnp.bfloat16)
        back_half = (dot(left_3a, diff_real) + dot(left_3b, diff_imag)).astype(jnp.bfloat16)
        back = dot(back_half[:side], right_4a) + dot(back_half[side:], right_4b)
        back_real = back[:, :side]
        back_imag = back[:, side:]
        filler = jnp.zeros((side, width - side), jnp.float32)
        below = jnp.zeros((8, width), jnp.float32)
        for part, value in enumerate(
            (
                probe_real * back_real + probe_imag * back_imag,
                probe_real * back_imag - probe_imag * back_real,
            )
        ):
            placed = pltpu.roll(jnp.concatenate([value, filler], axis=1), col, 1)
            placed = pltpu.roll(jnp.concatenate([placed, below], axis=0), row_shift, 0)
            grad_ref[part, rows, :] += placed
        probe_sum_ref[0] += patch_real * back_real + patch_imag * back_imag
        probe_sum_ref[1] += patch_real * back_imag - patch_imag * back_real
        energy = jnp.sum(patch_real * patch_real + patch_imag * patch_imag) / (side * side)
        energy_ref[...] += energy


def patch_terms_all(meta, window, amps, probe_field, tables):
    slots, side, _ = amps.shape
    full = lambda shape: pl.BlockSpec(shape, lambda slot, meta_ref: (0,) * len(shape))
    grid_spec = pltpu.PrefetchScalarGridSpec(
        num_scalar_prefetch=1,
        grid=(slots,),
        in_specs=[
            full(window.shape),
            pl.BlockSpec((1, side, side), lambda slot, meta_ref: (slot, 0, 0)),
            full((2, side, side)),
        ]
        + [full(table.shape) for table in tables],
        out_specs=[
            full(window.shape),
            full((2, side, side)),
            full((8, 128)),
        ],
    )
    return pl.pallas_call(
        patch_kernel,
        grid_spec=grid_spec,
        out_shape=[
            jax.ShapeDtypeStruct(window.shape, jnp.float32),
            jax.ShapeDtypeStruct((2, side, side), jnp.float32),
            jax.ShapeDtypeStruct((8, 128), jnp.float32),
        ],
        compiler_params=pltpu.CompilerParams(dimension_semantics=("arbitrary",)),
    )(meta, window, amps, probe_field, *tables)


def tile_edges(values, offset):
    return shifted(values, "tile", offset)


def on_device(
    object_field,
    probe_field,
    amplitudes,
    pos_rows,
    pos_cols,
    counts,
    admm_dual,
    volume,
    proj_weights,
    ray_weights,
    angle_ids,
):
    half_side = PB // 2
    own_object = object_field[0]
    tile_cols = own_object.shape[2]
    from_left = tile_edges(own_object[:, :, tile_cols - half_side :], 1)
    from_right = tile_edges(own_object[:, :, :half_side], -1)
    extended = jnp.concatenate([from_left, own_object, from_right], axis=2)
    dft_real, dft_imag = dft_tables(PB)
    probe_real = probe_field[0]
    probe_imag = probe_field[1]

    spare = -(-extended.shape[2] // 128) * 128 + 128 - extended.shape[2]
    window = jnp.pad(extended, ((0, 0), (0, 8), (0, spare)))
    meta = jnp.concatenate([counts[0, :1], pos_rows[0, 0], pos_cols[0, 0]])
    grad_sum, probe_sum, energy_rows = patch_terms_all(
        meta,
        window,
        amplitudes[0, 0],
        probe_field,
        stacked_tables(dft_real, dft_imag),
    )
    energy_sum = energy_rows[0, 0]
    grad_sum = grad_sum[:, : extended.shape[1]]
    to_right_edge = tile_edges(grad_sum[:, :, :half_side], -1)
    to_left_edge = tile_edges(grad_sum[:, :, tile_cols + half_side : tile_cols + PB], 1)
    own_cells = grad_sum[:, :, half_side : half_side + tile_cols]
    own_cells = own_cells.at[:, :, :half_side].add(to_left_edge)
    own_cells = own_cells.at[:, :, tile_cols - half_side :].add(to_right_edge)
    probe_order = link_order(bit_steps(("proj", "tile", "cuts")))
    probe_steps, probe_rest = probe_order[:3], probe_order[3:]
    probe_rows = probe_sum.size // 128
    padded_rows = -(-(probe_rows + 1) // 2 ** len(probe_steps)) * 2 ** len(probe_steps)
    probe_flat = jnp.concatenate(
        [
            probe_sum.reshape(probe_rows, 128),
            jnp.broadcast_to(energy_sum, (1, 128)),
            jnp.zeros((padded_rows - probe_rows - 1, 128), jnp.float32),
        ]
    )
    probe_chain = probe_ops(probe_steps, probe_rest)
    probe_peak = jnp.max(probe_real * probe_real + probe_imag * probe_imag)
    new_object = (own_object + own_cells / (probe_peak + 1e-05))[None]
    slab_total = admm_dual.shape[1]
    first_row = (own_object.shape[1] - slab_total) // 2
    slab_values = new_object[:, 1, first_row : first_row + slab_total, :] + admm_dual
    arrived = lax.all_to_all(
        lax.all_to_all(slab_values, "proj", split_axis=2, concat_axis=0, tiled=True),
        "cuts",
        split_axis=1,
        concat_axis=0,
        tiled=True,
    )
    proj_count = lax.axis_size("proj")
    cuts_count = lax.axis_size("cuts")
    slab_dev = arrived.shape[1]
    u_share = arrived.shape[2]
    projections = proj_count * cuts_count
    arrived = arrived.reshape(cuts_count, proj_count, slab_dev, u_share).transpose(1, 0, 2, 3)
    target = (
        arrived.reshape(projections, slab_dev, u_share)
        .transpose(2, 0, 1)
        .reshape(u_share, projections * slab_dev)
    )
    angle_count = ray_weights.shape[0]
    x_share = volume.shape[1]
    width = volume.shape[2]
    onehot = (angle_ids[:, None] == jnp.arange(angle_count, dtype=jnp.int32)[None, :]).astype(
        jnp.float32
    )
    ray_table = jnp.dot(
        onehot, ray_weights, precision=lax.Precision.HIGHEST, preferred_element_type=jnp.float32
    )
    ray_sums = jnp.einsum("zxy,ay->azx", volume, ray_table, precision=lax.Precision.HIGHEST).astype(
        jnp.bfloat16
    )
    spread = onehot.astype(jnp.bfloat16)[:, :, None, None] * ray_sums[:, None, :, :]
    spread = spread.transpose(1, 3, 0, 2).reshape(angle_count * x_share, projections * slab_dev)
    weight_flat = proj_weights.reshape(angle_count * x_share, width)
    partial_term = lax.dot_general(
        weight_flat, spread, (((0,), (0,)), ((), ())), preferred_element_type=jnp.float32
    )
    volume_steps = bit_steps(("tile", "proj"))
    volume_order = link_order(volume_steps)
    own_rows = ordered_scatter(partial_term, volume_steps, volume_order)
    own_residue = (own_rows - target).astype(jnp.bfloat16)
    gather_chain = [
        lambda values, step=step: doubling_step(values, *step, place=volume_steps.index(step))
        for step in reversed(volume_order)
    ]
    lead = len(probe_chain) - len(gather_chain)
    for operation in probe_chain[:lead]:
        probe_flat = operation(probe_flat)
    residue = own_residue.reshape((1,) * len(volume_steps) + own_residue.shape)
    for probe_op, gather_op in zip(probe_chain[lead:], gather_chain):
        probe_flat, residue = lax.optimization_barrier((probe_flat, residue))
        probe_flat = probe_op(probe_flat)
        residue = gather_op(residue)
    residue = residue.reshape((-1,) + residue.shape[len(volume_steps) + 1 :])
    probe_grad = probe_flat[:probe_rows].reshape(probe_sum.shape)
    energy = probe_flat[probe_rows, 0]
    new_probe = probe_field + probe_grad / (energy + 1e-05)
    backproj = matmul(weight_flat, residue)
    backproj = backproj.reshape(angle_count, x_share, projections, slab_dev)
    back_sums = jnp.einsum("gxaz,ag->azx", backproj, onehot, precision=lax.Precision.HIGHEST)
    gradient = jnp.einsum("azx,ay->zxy", back_sums, ray_table, precision=lax.Precision.HIGHEST)
    new_volume = volume - tomo_step * gradient
    return (new_object, new_probe, new_volume)


def solution(mesh):
    in_specs = (
        P(("proj", "cuts"), None, None, "tile"),
        P(),
        P(("proj", "cuts"), "tile", None, None, None),
        P(("proj", "cuts"), "tile", None),
        P(("proj", "cuts"), "tile", None),
        P(("proj", "cuts"), "tile"),
        P(("proj", "cuts"), None, "tile"),
        P("cuts", ("tile", "proj"), None),
        P(None, ("tile", "proj"), None),
        P(),
        P(),
    )
    out_specs = (P(("proj", "cuts"), None, None, "tile"), P(), P("cuts", ("tile", "proj"), None))
    return jax.shard_map(
        on_device, mesh=mesh, in_specs=in_specs, out_specs=out_specs, check_vma=False
    )
```

```python
import math

import jax
import jax.numpy as jnp
from jax import lax
from jax.experimental import pallas as pl
from jax.experimental.pallas import tpu as pltpu
from jax.sharding import PartitionSpec as P

PB = 256


tomo_step = 1.0


def shifted(value, axis, steps):
    count = lax.axis_size(axis)
    leading, last = (max(0, -steps), min(count, count - steps))
    return lax.ppermute(value, axis, [(source, source + steps) for source in range(leading, last)])


def dft_tables(side):
    indices = jnp.arange(side, dtype=jnp.int32)
    products = indices[:, None] * indices[None, :] % side
    phase_angle = products.astype(jnp.float32) * (2.0 * math.pi / side)
    norm_factor = 1.0 / math.sqrt(side)
    return (
        (jnp.cos(phase_angle) * norm_factor).astype(jnp.bfloat16),
        (-jnp.sin(phase_angle) * norm_factor).astype(jnp.bfloat16),
    )


def matmul(left, right):
    return jnp.dot(left, right, preferred_element_type=jnp.float32)


def complex_matmul(left_real, left_imag, right_real, right_imag):
    out_real = matmul(left_real, right_real) - matmul(left_imag, right_imag)
    out_imag = matmul(left_real, right_imag) + matmul(left_imag, right_real)
    return (out_real, out_imag)


def patch_terms(patch_real, patch_imag, probe_real, probe_imag, amplitude, dft_real, dft_imag):
    wave_real = (probe_real * patch_real - probe_imag * patch_imag).astype(jnp.bfloat16)
    wave_imag = (probe_real * patch_imag + probe_imag * patch_real).astype(jnp.bfloat16)
    half_real, half_imag = complex_matmul(dft_real, dft_imag, wave_real, wave_imag)
    half_real = half_real.astype(jnp.bfloat16)
    half_imag = half_imag.astype(jnp.bfloat16)
    far_real, far_imag = complex_matmul(half_real, half_imag, dft_real, dft_imag)
    modulus = jnp.sqrt(far_real * far_real + far_imag * far_imag + 0.25)
    factor = amplitude.astype(jnp.float32) / modulus - 1.0
    diff_real = (far_real * factor).astype(jnp.bfloat16)
    diff_imag = (far_imag * factor).astype(jnp.bfloat16)
    conj_imag = -dft_imag
    back_half_real, back_half_imag = complex_matmul(dft_real, conj_imag, diff_real, diff_imag)
    back_half_real = back_half_real.astype(jnp.bfloat16)
    back_half_imag = back_half_imag.astype(jnp.bfloat16)
    back_real, back_imag = complex_matmul(back_half_real, back_half_imag, dft_real, conj_imag)
    object_real = probe_real * back_real + probe_imag * back_imag
    object_imag = probe_real * back_imag - probe_imag * back_real
    probe_grad_real = patch_real * back_real + patch_imag * back_imag
    probe_grad_imag = patch_real * back_imag - patch_imag * back_real
    energy = jnp.mean(patch_real * patch_real + patch_imag * patch_imag)
    return (
        jnp.stack([object_real, object_imag]),
        jnp.stack([probe_grad_real, probe_grad_imag]),
        energy,
    )


def axis_bits(axis):
    return lax.axis_size(axis).bit_length() - 1


def bit_steps(axes):
    steps = []
    for axis in axes:
        steps += [(axis, bit) for bit in reversed(range(axis_bits(axis)))]
    return steps


def link_order(steps):
    by_distance = [("proj", 0), ("tile", 0), ("cuts", 0), ("proj", 2), ("tile", 1), ("cuts", 1)]
    ranked = [step for step in by_distance if step in steps]
    return ranked + [step for step in steps if step not in ranked]


def bit_view(values, steps):
    return values.reshape((2,) * len(steps) + (values.shape[0] >> len(steps),) + values.shape[1:])


def ordered_scatter(values, steps, order):
    values = bit_view(values, steps)
    for axis, bit in order:
        place = steps.index((axis, bit))
        mine = (lax.axis_index(axis) >> bit) & 1
        keep = lax.dynamic_slice_in_dim(values, mine, 1, place)
        send = lax.dynamic_slice_in_dim(values, 1 - mine, 1, place)
        values = keep + exchange(send, axis, bit)
    return values.reshape(values.shape[len(steps) :])


def ordered_gather(values, steps, order):
    values = values.reshape((1,) * len(steps) + values.shape)
    for axis, bit in reversed(order):
        place = steps.index((axis, bit))
        mine = (lax.axis_index(axis) >> bit) & 1
        other = exchange(values, axis, bit)
        values = jnp.where(
            mine == 0,
            jnp.concatenate([values, other], axis=place),
            jnp.concatenate([other, values], axis=place),
        )
    return values.reshape((-1,) + values.shape[len(steps) + 1 :])


def exchange(values, axis, bit):
    count = lax.axis_size(axis)
    return lax.ppermute(values, axis, [(source, source ^ (1 << bit)) for source in range(count)])


def halving_scatter(values, steps):
    for axis, bit in steps:
        mine = (lax.axis_index(axis) >> bit) & 1
        half = values.shape[0] // 2
        keep = lax.dynamic_slice_in_dim(values, mine * half, half, 0)
        send = lax.dynamic_slice_in_dim(values, (1 - mine) * half, half, 0)
        values = keep + exchange(send, axis, bit)
    return values


def exchange_sum(values, steps):
    for axis, bit in steps:
        values = values + exchange(values, axis, bit)
    return values


def doubling_gather(values, steps):
    for axis, bit in reversed(steps):
        mine = (lax.axis_index(axis) >> bit) & 1
        other = exchange(values, axis, bit)
        values = jnp.where(
            mine == 0,
            jnp.concatenate([values, other], axis=0),
            jnp.concatenate([other, values], axis=0),
        )
    return values


def stacked_tables(dft_real, dft_imag):
    rows = lambda top, bottom: jnp.concatenate([top, bottom], axis=0)
    cols = lambda left, right: jnp.concatenate([left, right], axis=1)
    return (
        rows(dft_real, dft_imag),
        rows(-dft_imag, dft_real),
        cols(dft_real, dft_imag),
        cols(-dft_imag, dft_real),
        rows(dft_real, -dft_imag),
        rows(dft_imag, dft_real),
        cols(dft_real, -dft_imag),
        cols(dft_imag, dft_real),
    )


def patch_kernel(meta_ref, window_ref, amp_ref, probe_ref, *refs):
    tables = refs[:8]
    grad_ref, probe_sum_ref, energy_ref = refs[8:]
    slot = pl.program_id(0)
    slots = pl.num_programs(0)
    side = probe_ref.shape[1]

    @pl.when(slot == 0)
    def _():
        grad_ref[...] = jnp.zeros(grad_ref.shape, jnp.float32)
        probe_sum_ref[...] = jnp.zeros(probe_sum_ref.shape, jnp.float32)
        energy_ref[...] = jnp.zeros(energy_ref.shape, jnp.float32)

    @pl.when(slot < meta_ref[0])
    def _():
        row = meta_ref[1 + slot]
        col = meta_ref[1 + slots + slot]
        band = side + 8
        rows = pl.ds(pl.multiple_of(row // 8 * 8, 8), band)
        row_shift = row % 8
        span = side + 128
        cols = pl.ds(pl.multiple_of(col // 128 * 128, 128), span)
        col_shift = col % 128
        to_front = (span - col_shift) % span

        def extract(part):
            values = pltpu.roll(window_ref[part, rows, cols], (band - row_shift) % band, 0)
            return pltpu.roll(values[:side], to_front, 1)[:, :side]

        patch_real = extract(0)
        patch_imag = extract(1)
        dot = lambda left, right: jnp.dot(left, right, preferred_element_type=jnp.float32)
        left_1a, left_1b, right_2a, right_2b, left_3a, left_3b, right_4a, right_4b = (
            table[...] for table in tables
        )
        probe_real = probe_ref[0]
        probe_imag = probe_ref[1]
        wave_real = (probe_real * patch_real - probe_imag * patch_imag).astype(jnp.bfloat16)
        wave_imag = (probe_real * patch_imag + probe_imag * patch_real).astype(jnp.bfloat16)
        half = (dot(left_1a, wave_real) + dot(left_1b, wave_imag)).astype(jnp.bfloat16)
        far = dot(half[:side], right_2a) + dot(half[side:], right_2b)
        far_real = far[:, :side]
        far_imag = far[:, side:]
        modulus = jnp.sqrt(far_real * far_real + far_imag * far_imag + 0.25)
        factor = amp_ref[0].astype(jnp.float32) / modulus - 1.0
        diff_real = (far_real * factor).astype(jnp.bfloat16)
        diff_imag = (far_imag * factor).astype(jnp.bfloat16)
        back_half = (dot(left_3a, diff_real) + dot(left_3b, diff_imag)).astype(jnp.bfloat16)
        back = dot(back_half[:side], right_4a) + dot(back_half[side:], right_4b)
        back_real = back[:, :side]
        back_imag = back[:, side:]
        filler = jnp.zeros((side, span - side), jnp.float32)
        below = jnp.zeros((8, span), jnp.float32)
        for part, value in enumerate(
            (
                probe_real * back_real + probe_imag * back_imag,
                probe_real * back_imag - probe_imag * back_real,
            )
        ):
            placed = pltpu.roll(jnp.concatenate([value, filler], axis=1), col_shift, 1)
            placed = pltpu.roll(jnp.concatenate([placed, below], axis=0), row_shift, 0)
            grad_ref[part, rows, cols] += placed
        probe_sum_ref[0] += patch_real * back_real + patch_imag * back_imag
        probe_sum_ref[1] += patch_real * back_imag - patch_imag * back_real
        energy = jnp.sum(patch_real * patch_real + patch_imag * patch_imag) / (side * side)
        energy_ref[...] += energy


def patch_terms_all(meta, window, amps, probe_field, tables):
    slots, side, _ = amps.shape
    full = lambda shape: pl.BlockSpec(shape, lambda slot, meta_ref: (0,) * len(shape))
    grid_spec = pltpu.PrefetchScalarGridSpec(
        num_scalar_prefetch=1,
        grid=(slots,),
        in_specs=[
            full(window.shape),
            pl.BlockSpec((1, side, side), lambda slot, meta_ref: (slot, 0, 0)),
            full((2, side, side)),
        ]
        + [full(table.shape) for table in tables],
        out_specs=[
            full(window.shape),
            full((2, side, side)),
            full((8, 128)),
        ],
    )
    return pl.pallas_call(
        patch_kernel,
        grid_spec=grid_spec,
        out_shape=[
            jax.ShapeDtypeStruct(window.shape, jnp.float32),
            jax.ShapeDtypeStruct((2, side, side), jnp.float32),
            jax.ShapeDtypeStruct((8, 128), jnp.float32),
        ],
        compiler_params=pltpu.CompilerParams(dimension_semantics=("arbitrary",)),
    )(meta, window, amps, probe_field, *tables)


def tile_edges(values, offset):
    return shifted(values, "tile", offset)


def on_device(
    object_field,
    probe_field,
    amplitudes,
    pos_rows,
    pos_cols,
    counts,
    admm_dual,
    volume,
    proj_weights,
    ray_weights,
    angle_ids,
):
    half_side = PB // 2
    own_object = object_field[0]
    tile_cols = own_object.shape[2]
    from_left = tile_edges(own_object[:, :, tile_cols - half_side :], 1)
    from_right = tile_edges(own_object[:, :, :half_side], -1)
    extended = jnp.concatenate([from_left, own_object, from_right], axis=2)
    dft_real, dft_imag = dft_tables(PB)
    probe_real = probe_field[0]
    probe_imag = probe_field[1]

    spare = -(-extended.shape[2] // 128) * 128 + 128 - extended.shape[2]
    window = jnp.pad(extended, ((0, 0), (0, 8), (0, spare)))
    meta = jnp.concatenate([counts[0, :1], pos_rows[0, 0], pos_cols[0, 0]])
    grad_sum, probe_sum, energy_rows = patch_terms_all(
        meta,
        window,
        amplitudes[0, 0],
        probe_field,
        stacked_tables(dft_real, dft_imag),
    )
    energy_sum = energy_rows[0, 0]
    grad_sum = grad_sum[:, : extended.shape[1]]
    to_right_edge = tile_edges(grad_sum[:, :, :half_side], -1)
    to_left_edge = tile_edges(grad_sum[:, :, tile_cols + half_side : tile_cols + PB], 1)
    own_cells = grad_sum[:, :, half_side : half_side + tile_cols]
    own_cells = own_cells.at[:, :, :half_side].add(to_left_edge)
    own_cells = own_cells.at[:, :, tile_cols - half_side :].add(to_right_edge)
    probe_order = link_order(bit_steps(("proj", "tile", "cuts")))
    probe_steps, probe_rest = probe_order[:3], probe_order[3:]
    probe_rows = probe_sum.size // 128
    padded_rows = -(-(probe_rows + 1) // 2 ** len(probe_steps)) * 2 ** len(probe_steps)
    probe_flat = jnp.concatenate(
        [
            probe_sum.reshape(probe_rows, 128),
            jnp.broadcast_to(energy_sum, (1, 128)),
            jnp.zeros((padded_rows - probe_rows - 1, 128), jnp.float32),
        ]
    )
    probe_flat = exchange_sum(halving_scatter(probe_flat, probe_steps), probe_rest)
    probe_flat = doubling_gather(probe_flat, probe_steps)
    probe_grad = probe_flat[:probe_rows].reshape(probe_sum.shape)
    energy = probe_flat[probe_rows, 0]
    new_probe = probe_field + probe_grad / (energy + 1e-05)
    probe_peak = jnp.max(probe_real * probe_real + probe_imag * probe_imag)
    new_object = (own_object + own_cells / (probe_peak + 1e-05))[None]
    slab_total = admm_dual.shape[1]
    first_row = (own_object.shape[1] - slab_total) // 2
    slab_values = new_object[:, 1, first_row : first_row + slab_total, :] + admm_dual
    arrived = lax.all_to_all(
        lax.all_to_all(slab_values, "proj", split_axis=2, concat_axis=0, tiled=True),
        "cuts",
        split_axis=1,
        concat_axis=0,
        tiled=True,
    )
    proj_count = lax.axis_size("proj")
    cuts_count = lax.axis_size("cuts")
    slab_dev = arrived.shape[1]
    u_share = arrived.shape[2]
    projections = proj_count * cuts_count
    arrived = arrived.reshape(cuts_count, proj_count, slab_dev, u_share).transpose(1, 0, 2, 3)
    target = (
        arrived.reshape(projections, slab_dev, u_share)
        .transpose(2, 0, 1)
        .reshape(u_share, projections * slab_dev)
    )
    angle_count = ray_weights.shape[0]
    x_share = volume.shape[1]
    width = volume.shape[2]
    onehot = (angle_ids[:, None] == jnp.arange(angle_count, dtype=jnp.int32)[None, :]).astype(
        jnp.float32
    )
    ray_table = jnp.dot(
        onehot, ray_weights, precision=lax.Precision.HIGHEST, preferred_element_type=jnp.float32
    )
    ray_sums = jnp.einsum("zxy,ay->azx", volume, ray_table, precision=lax.Precision.HIGHEST).astype(
        jnp.bfloat16
    )
    spread = onehot.astype(jnp.bfloat16)[:, :, None, None] * ray_sums[:, None, :, :]
    spread = spread.transpose(1, 3, 0, 2).reshape(angle_count * x_share, projections * slab_dev)
    weight_flat = proj_weights.reshape(angle_count * x_share, width)
    partial_term = lax.dot_general(
        weight_flat, spread, (((0,), (0,)), ((), ())), preferred_element_type=jnp.float32
    )
    volume_steps = bit_steps(("tile", "proj"))
    volume_order = link_order(volume_steps)
    own_rows = ordered_scatter(partial_term, volume_steps, volume_order)
    own_residue = (own_rows - target).astype(jnp.bfloat16)
    residue = ordered_gather(own_residue, volume_steps, volume_order)
    backproj = matmul(weight_flat, residue)
    backproj = backproj.reshape(angle_count, x_share, projections, slab_dev)
    back_sums = jnp.einsum("gxaz,ag->azx", backproj, onehot, precision=lax.Precision.HIGHEST)
    gradient = jnp.einsum("azx,ay->zxy", back_sums, ray_table, precision=lax.Precision.HIGHEST)
    new_volume = volume - tomo_step * gradient
    return (new_object, new_probe, new_volume)


def solution(mesh):
    in_specs = (
        P(("proj", "cuts"), None, None, "tile"),
        P(),
        P(("proj", "cuts"), "tile", None, None, None),
        P(("proj", "cuts"), "tile", None),
        P(("proj", "cuts"), "tile", None),
        P(("proj", "cuts"), "tile"),
        P(("proj", "cuts"), None, "tile"),
        P("cuts", ("tile", "proj"), None),
        P(None, ("tile", "proj"), None),
        P(),
        P(),
    )
    out_specs = (P(("proj", "cuts"), None, None, "tile"), P(), P("cuts", ("tile", "proj"), None))
    return jax.shard_map(
        on_device, mesh=mesh, in_specs=in_specs, out_specs=out_specs, check_vma=False
    )
```

```python
import math

import jax
import jax.numpy as jnp
from jax import lax
from jax.experimental import pallas as pl
from jax.experimental.pallas import tpu as pltpu
from jax.sharding import PartitionSpec as P

PB = 256


tomo_step = 1.0


def shifted(value, axis, steps):
    count = lax.axis_size(axis)
    leading, last = (max(0, -steps), min(count, count - steps))
    return lax.ppermute(value, axis, [(source, source + steps) for source in range(leading, last)])


def dft_tables(side):
    indices = jnp.arange(side, dtype=jnp.int32)
    products = indices[:, None] * indices[None, :] % side
    phase_angle = products.astype(jnp.float32) * (2.0 * math.pi / side)
    norm_factor = 1.0 / math.sqrt(side)
    return (
        (jnp.cos(phase_angle) * norm_factor).astype(jnp.bfloat16),
        (-jnp.sin(phase_angle) * norm_factor).astype(jnp.bfloat16),
    )


def matmul(left, right):
    return jnp.dot(left, right, preferred_element_type=jnp.float32)


def complex_matmul(left_real, left_imag, right_real, right_imag):
    out_real = matmul(left_real, right_real) - matmul(left_imag, right_imag)
    out_imag = matmul(left_real, right_imag) + matmul(left_imag, right_real)
    return (out_real, out_imag)


def patch_terms(patch_real, patch_imag, probe_real, probe_imag, amplitude, dft_real, dft_imag):
    wave_real = (probe_real * patch_real - probe_imag * patch_imag).astype(jnp.bfloat16)
    wave_imag = (probe_real * patch_imag + probe_imag * patch_real).astype(jnp.bfloat16)
    half_real, half_imag = complex_matmul(dft_real, dft_imag, wave_real, wave_imag)
    half_real = half_real.astype(jnp.bfloat16)
    half_imag = half_imag.astype(jnp.bfloat16)
    far_real, far_imag = complex_matmul(half_real, half_imag, dft_real, dft_imag)
    modulus = jnp.sqrt(far_real * far_real + far_imag * far_imag + 0.25)
    factor = amplitude.astype(jnp.float32) / modulus - 1.0
    diff_real = (far_real * factor).astype(jnp.bfloat16)
    diff_imag = (far_imag * factor).astype(jnp.bfloat16)
    conj_imag = -dft_imag
    back_half_real, back_half_imag = complex_matmul(dft_real, conj_imag, diff_real, diff_imag)
    back_half_real = back_half_real.astype(jnp.bfloat16)
    back_half_imag = back_half_imag.astype(jnp.bfloat16)
    back_real, back_imag = complex_matmul(back_half_real, back_half_imag, dft_real, conj_imag)
    object_real = probe_real * back_real + probe_imag * back_imag
    object_imag = probe_real * back_imag - probe_imag * back_real
    probe_grad_real = patch_real * back_real + patch_imag * back_imag
    probe_grad_imag = patch_real * back_imag - patch_imag * back_real
    energy = jnp.mean(patch_real * patch_real + patch_imag * patch_imag)
    return (
        jnp.stack([object_real, object_imag]),
        jnp.stack([probe_grad_real, probe_grad_imag]),
        energy,
    )


def axis_bits(axis):
    return lax.axis_size(axis).bit_length() - 1


def bit_steps(axes):
    steps = []
    for axis in axes:
        steps += [(axis, bit) for bit in reversed(range(axis_bits(axis)))]
    return steps


def link_order(steps):
    by_distance = [("proj", 0), ("tile", 0), ("cuts", 0), ("proj", 2), ("tile", 1), ("cuts", 1)]
    ranked = [step for step in by_distance if step in steps]
    return ranked + [step for step in steps if step not in ranked]


def bit_view(values, steps):
    return values.reshape((2,) * len(steps) + (values.shape[0] >> len(steps),) + values.shape[1:])


def ordered_scatter(values, steps, order):
    values = bit_view(values, steps)
    for axis, bit in order:
        place = steps.index((axis, bit))
        mine = (lax.axis_index(axis) >> bit) & 1
        keep = lax.dynamic_slice_in_dim(values, mine, 1, place)
        send = lax.dynamic_slice_in_dim(values, 1 - mine, 1, place)
        values = keep + exchange(send, axis, bit)
    return values.reshape(values.shape[len(steps) :])


def ordered_gather(values, steps, order):
    values = values.reshape((1,) * len(steps) + values.shape)
    for axis, bit in reversed(order):
        place = steps.index((axis, bit))
        mine = (lax.axis_index(axis) >> bit) & 1
        other = exchange(values, axis, bit)
        values = jnp.where(
            mine == 0,
            jnp.concatenate([values, other], axis=place),
            jnp.concatenate([other, values], axis=place),
        )
    return values.reshape((-1,) + values.shape[len(steps) + 1 :])


def exchange(values, axis, bit):
    count = lax.axis_size(axis)
    return lax.ppermute(values, axis, [(source, source ^ (1 << bit)) for source in range(count)])


def halving_scatter(values, steps):
    for axis, bit in steps:
        mine = (lax.axis_index(axis) >> bit) & 1
        half = values.shape[0] // 2
        keep = lax.dynamic_slice_in_dim(values, mine * half, half, 0)
        send = lax.dynamic_slice_in_dim(values, (1 - mine) * half, half, 0)
        values = keep + exchange(send, axis, bit)
    return values


def exchange_sum(values, steps):
    for axis, bit in steps:
        values = values + exchange(values, axis, bit)
    return values


def doubling_gather(values, steps):
    for axis, bit in reversed(steps):
        mine = (lax.axis_index(axis) >> bit) & 1
        other = exchange(values, axis, bit)
        values = jnp.where(
            mine == 0,
            jnp.concatenate([values, other], axis=0),
            jnp.concatenate([other, values], axis=0),
        )
    return values


def stacked_tables(dft_real, dft_imag):
    rows = lambda top, bottom: jnp.concatenate([top, bottom], axis=0)
    cols = lambda left, right: jnp.concatenate([left, right], axis=1)
    return (
        rows(dft_real, dft_imag),
        rows(-dft_imag, dft_real),
        cols(dft_real, dft_imag),
        cols(-dft_imag, dft_real),
        rows(dft_real, -dft_imag),
        rows(dft_imag, dft_real),
        cols(dft_real, -dft_imag),
        cols(dft_imag, dft_real),
    )


def patch_kernel(meta_ref, window_ref, amp_ref, probe_ref, *refs):
    tables = refs[:8]
    grad_ref, probe_sum_ref, energy_ref = refs[8:]
    slot = pl.program_id(0)
    slots = pl.num_programs(0)
    side = probe_ref.shape[1]

    @pl.when(slot == 0)
    def _():
        grad_ref[...] = jnp.zeros(grad_ref.shape, jnp.float32)
        probe_sum_ref[...] = jnp.zeros(probe_sum_ref.shape, jnp.float32)
        energy_ref[...] = jnp.zeros(energy_ref.shape, jnp.float32)

    @pl.when(slot < meta_ref[0])
    def _():
        row = meta_ref[1 + slot]
        col = meta_ref[1 + slots + slot]
        band = side + 8
        rows = pl.ds(pl.multiple_of(row // 8 * 8, 8), band)
        row_shift = row % 8
        span = side + 128
        cols = pl.ds(pl.multiple_of(col // 128 * 128, 128), span)
        col_shift = col % 128
        to_front = (span - col_shift) % span

        def extract(part):
            values = pltpu.roll(window_ref[part, rows, cols], (band - row_shift) % band, 0)
            return pltpu.roll(values[:side], to_front, 1)[:, :side]

        patch_real = extract(0)
        patch_imag = extract(1)
        dot = lambda left, right: jnp.dot(left, right, preferred_element_type=jnp.float32)
        left_1a, left_1b, right_2a, right_2b, left_3a, left_3b, right_4a, right_4b = (
            table[...] for table in tables
        )
        probe_real = probe_ref[0]
        probe_imag = probe_ref[1]
        wave_real = (probe_real * patch_real - probe_imag * patch_imag).astype(jnp.bfloat16)
        wave_imag = (probe_real * patch_imag + probe_imag * patch_real).astype(jnp.bfloat16)
        half = (dot(left_1a, wave_real) + dot(left_1b, wave_imag)).astype(jnp.bfloat16)
        far = dot(half[:side], right_2a) + dot(half[side:], right_2b)
        far_real = far[:, :side]
        far_imag = far[:, side:]
        modulus = jnp.sqrt(far_real * far_real + far_imag * far_imag + 0.25)
        factor = amp_ref[0].astype(jnp.float32) / modulus - 1.0
        diff_real = (far_real * factor).astype(jnp.bfloat16)
        diff_imag = (far_imag * factor).astype(jnp.bfloat16)
        back_half = (dot(left_3a, diff_real) + dot(left_3b, diff_imag)).astype(jnp.bfloat16)
        back = dot(back_half[:side], right_4a) + dot(back_half[side:], right_4b)
        back_real = back[:, :side]
        back_imag = back[:, side:]
        filler = jnp.zeros((side, span - side), jnp.float32)
        below = jnp.zeros((8, span), jnp.float32)
        for part, value in enumerate(
            (
                probe_real * back_real + probe_imag * back_imag,
                probe_real * back_imag - probe_imag * back_real,
            )
        ):
            placed = pltpu.roll(jnp.concatenate([value, filler], axis=1), col_shift, 1)
            placed = pltpu.roll(jnp.concatenate([placed, below], axis=0), row_shift, 0)
            grad_ref[part, rows, cols] += placed
        probe_sum_ref[0] += patch_real * back_real + patch_imag * back_imag
        probe_sum_ref[1] += patch_real * back_imag - patch_imag * back_real
        energy = jnp.sum(patch_real * patch_real + patch_imag * patch_imag) / (side * side)
        energy_ref[...] += energy


def patch_terms_all(meta, window, amps, probe_field, tables):
    slots, side, _ = amps.shape
    full = lambda shape: pl.BlockSpec(shape, lambda slot, meta_ref: (0,) * len(shape))
    grid_spec = pltpu.PrefetchScalarGridSpec(
        num_scalar_prefetch=1,
        grid=(slots,),
        in_specs=[
            full(window.shape),
            pl.BlockSpec((1, side, side), lambda slot, meta_ref: (slot, 0, 0)),
            full((2, side, side)),
        ]
        + [full(table.shape) for table in tables],
        out_specs=[
            full(window.shape),
            full((2, side, side)),
            full((8, 128)),
        ],
    )
    return pl.pallas_call(
        patch_kernel,
        grid_spec=grid_spec,
        out_shape=[
            jax.ShapeDtypeStruct(window.shape, jnp.float32),
            jax.ShapeDtypeStruct((2, side, side), jnp.float32),
            jax.ShapeDtypeStruct((8, 128), jnp.float32),
        ],
        compiler_params=pltpu.CompilerParams(dimension_semantics=("arbitrary",)),
    )(meta, window, amps, probe_field, *tables)


def tile_edges(values, offset):
    return shifted(values, "tile", offset)


def on_device(
    object_field,
    probe_field,
    amplitudes,
    pos_rows,
    pos_cols,
    counts,
    admm_dual,
    volume,
    proj_weights,
    ray_weights,
    angle_ids,
):
    half_side = PB // 2
    own_object = object_field[0]
    tile_cols = own_object.shape[2]
    from_left = tile_edges(own_object[:, :, tile_cols - half_side :], 1)
    from_right = tile_edges(own_object[:, :, :half_side], -1)
    extended = jnp.concatenate([from_left, own_object, from_right], axis=2)
    dft_real, dft_imag = dft_tables(PB)
    probe_real = probe_field[0]
    probe_imag = probe_field[1]

    spare = -(-extended.shape[2] // 128) * 128 + 128 - extended.shape[2]
    window = jnp.pad(extended, ((0, 0), (0, 8), (0, spare)))
    meta = jnp.concatenate([counts[0, :1], pos_rows[0, 0], pos_cols[0, 0]])
    grad_sum, probe_sum, energy_rows = patch_terms_all(
        meta,
        window,
        amplitudes[0, 0],
        probe_field,
        stacked_tables(dft_real, dft_imag),
    )
    energy_sum = energy_rows[0, 0]
    grad_sum = grad_sum[:, : extended.shape[1]]
    to_right_edge = tile_edges(grad_sum[:, :, :half_side], -1)
    to_left_edge = tile_edges(grad_sum[:, :, tile_cols + half_side : tile_cols + PB], 1)
    own_cells = grad_sum[:, :, half_side : half_side + tile_cols]
    own_cells = own_cells.at[:, :, :half_side].add(to_left_edge)
    own_cells = own_cells.at[:, :, tile_cols - half_side :].add(to_right_edge)
    probe_order = link_order(bit_steps(("proj", "tile", "cuts")))
    probe_steps, probe_rest = probe_order[:3], probe_order[3:]
    probe_rows = probe_sum.size // 128
    padded_rows = -(-(probe_rows + 1) // 2 ** len(probe_steps)) * 2 ** len(probe_steps)
    probe_flat = jnp.concatenate(
        [
            probe_sum.reshape(probe_rows, 128),
            jnp.broadcast_to(energy_sum, (1, 128)),
            jnp.zeros((padded_rows - probe_rows - 1, 128), jnp.float32),
        ]
    )
    probe_flat = exchange_sum(halving_scatter(probe_flat, probe_steps), probe_rest)
    probe_flat = doubling_gather(probe_flat, probe_steps)
    probe_grad = probe_flat[:probe_rows].reshape(probe_sum.shape)
    energy = probe_flat[probe_rows, 0]
    new_probe = probe_field + probe_grad / (energy + 1e-05)
    probe_peak = jnp.max(probe_real * probe_real + probe_imag * probe_imag)
    new_object = (own_object + own_cells / (probe_peak + 1e-05))[None]
    slab_total = admm_dual.shape[1]
    first_row = (own_object.shape[1] - slab_total) // 2
    slab_values = new_object[:, 1, first_row : first_row + slab_total, :] + admm_dual
    arrived = lax.all_to_all(
        lax.all_to_all(slab_values, "proj", split_axis=2, concat_axis=0, tiled=True),
        "cuts",
        split_axis=1,
        concat_axis=0,
        tiled=True,
    )
    proj_count = lax.axis_size("proj")
    cuts_count = lax.axis_size("cuts")
    slab_dev = arrived.shape[1]
    u_share = arrived.shape[2]
    projections = proj_count * cuts_count
    arrived = arrived.reshape(cuts_count, proj_count, slab_dev, u_share).transpose(1, 0, 2, 3)
    target = (
        arrived.reshape(projections, slab_dev, u_share)
        .transpose(2, 0, 1)
        .reshape(u_share, projections * slab_dev)
    )
    angle_count = ray_weights.shape[0]
    x_share = volume.shape[1]
    width = volume.shape[2]
    onehot = (angle_ids[:, None] == jnp.arange(angle_count, dtype=jnp.int32)[None, :]).astype(
        jnp.float32
    )
    ray_table = jnp.dot(
        onehot, ray_weights, precision=lax.Precision.HIGHEST, preferred_element_type=jnp.float32
    )
    ray_sums = jnp.einsum("zxy,ay->azx", volume, ray_table, precision=lax.Precision.HIGHEST).astype(
        jnp.bfloat16
    )
    spread = onehot.astype(jnp.bfloat16)[:, :, None, None] * ray_sums[:, None, :, :]
    spread = spread.transpose(1, 3, 0, 2).reshape(angle_count * x_share, projections * slab_dev)
    weight_flat = proj_weights.reshape(angle_count * x_share, width)
    partial_term = lax.dot_general(
        weight_flat, spread, (((0,), (0,)), ((), ())), preferred_element_type=jnp.float32
    )
    volume_steps = bit_steps(("tile", "proj"))
    volume_order = link_order(volume_steps)
    own_rows = ordered_scatter(partial_term, volume_steps, volume_order)
    own_residue = (own_rows - target).astype(jnp.bfloat16)
    residue = ordered_gather(own_residue, volume_steps, volume_order)
    backproj = matmul(weight_flat, residue)
    backproj = backproj.reshape(angle_count, x_share, projections, slab_dev)
    back_sums = jnp.sum(backproj * onehot.T[:, None, :, None], axis=0).transpose(1, 2, 0)
    gradient = jnp.einsum("azx,ay->zxy", back_sums, ray_table, precision=lax.Precision.HIGHEST)
    new_volume = volume - tomo_step * gradient
    return (new_object, new_probe, new_volume)


def solution(mesh):
    in_specs = (
        P(("proj", "cuts"), None, None, "tile"),
        P(),
        P(("proj", "cuts"), "tile", None, None, None),
        P(("proj", "cuts"), "tile", None),
        P(("proj", "cuts"), "tile", None),
        P(("proj", "cuts"), "tile"),
        P(("proj", "cuts"), None, "tile"),
        P("cuts", ("tile", "proj"), None),
        P(None, ("tile", "proj"), None),
        P(),
        P(),
    )
    out_specs = (P(("proj", "cuts"), None, None, "tile"), P(), P("cuts", ("tile", "proj"), None))
    return jax.shard_map(
        on_device, mesh=mesh, in_specs=in_specs, out_specs=out_specs, check_vma=False
    )
```

```python
import math

import jax
import jax.numpy as jnp
from jax import lax
from jax.experimental import pallas as pl
from jax.experimental.pallas import tpu as pltpu
from jax.sharding import PartitionSpec as P

PB = 256


tomo_step = 1.0


def shifted(value, axis, steps):
    count = lax.axis_size(axis)
    leading, last = (max(0, -steps), min(count, count - steps))
    return lax.ppermute(value, axis, [(source, source + steps) for source in range(leading, last)])


def dft_tables(side):
    indices = jnp.arange(side, dtype=jnp.int32)
    products = indices[:, None] * indices[None, :] % side
    phase_angle = products.astype(jnp.float32) * (2.0 * math.pi / side)
    norm_factor = 1.0 / math.sqrt(side)
    return (
        (jnp.cos(phase_angle) * norm_factor).astype(jnp.bfloat16),
        (-jnp.sin(phase_angle) * norm_factor).astype(jnp.bfloat16),
    )


def matmul(left, right):
    return jnp.dot(left, right, preferred_element_type=jnp.float32)


def complex_matmul(left_real, left_imag, right_real, right_imag):
    out_real = matmul(left_real, right_real) - matmul(left_imag, right_imag)
    out_imag = matmul(left_real, right_imag) + matmul(left_imag, right_real)
    return (out_real, out_imag)


def patch_terms(patch_real, patch_imag, probe_real, probe_imag, amplitude, dft_real, dft_imag):
    wave_real = (probe_real * patch_real - probe_imag * patch_imag).astype(jnp.bfloat16)
    wave_imag = (probe_real * patch_imag + probe_imag * patch_real).astype(jnp.bfloat16)
    half_real, half_imag = complex_matmul(dft_real, dft_imag, wave_real, wave_imag)
    half_real = half_real.astype(jnp.bfloat16)
    half_imag = half_imag.astype(jnp.bfloat16)
    far_real, far_imag = complex_matmul(half_real, half_imag, dft_real, dft_imag)
    modulus = jnp.sqrt(far_real * far_real + far_imag * far_imag + 0.25)
    factor = amplitude.astype(jnp.float32) / modulus - 1.0
    diff_real = (far_real * factor).astype(jnp.bfloat16)
    diff_imag = (far_imag * factor).astype(jnp.bfloat16)
    conj_imag = -dft_imag
    back_half_real, back_half_imag = complex_matmul(dft_real, conj_imag, diff_real, diff_imag)
    back_half_real = back_half_real.astype(jnp.bfloat16)
    back_half_imag = back_half_imag.astype(jnp.bfloat16)
    back_real, back_imag = complex_matmul(back_half_real, back_half_imag, dft_real, conj_imag)
    object_real = probe_real * back_real + probe_imag * back_imag
    object_imag = probe_real * back_imag - probe_imag * back_real
    probe_grad_real = patch_real * back_real + patch_imag * back_imag
    probe_grad_imag = patch_real * back_imag - patch_imag * back_real
    energy = jnp.mean(patch_real * patch_real + patch_imag * patch_imag)
    return (
        jnp.stack([object_real, object_imag]),
        jnp.stack([probe_grad_real, probe_grad_imag]),
        energy,
    )


def axis_bits(axis):
    return lax.axis_size(axis).bit_length() - 1


def bit_steps(axes):
    steps = []
    for axis in axes:
        steps += [(axis, bit) for bit in reversed(range(axis_bits(axis)))]
    return steps


def link_order(steps):
    by_distance = [("proj", 0), ("tile", 0), ("cuts", 0), ("proj", 2), ("tile", 1), ("cuts", 1)]
    ranked = [step for step in by_distance if step in steps]
    return ranked + [step for step in steps if step not in ranked]


def bit_view(values, steps):
    return values.reshape((2,) * len(steps) + (values.shape[0] >> len(steps),) + values.shape[1:])


def ordered_scatter(values, steps, order):
    values = bit_view(values, steps)
    for axis, bit in order:
        place = steps.index((axis, bit))
        mine = (lax.axis_index(axis) >> bit) & 1
        keep = lax.dynamic_slice_in_dim(values, mine, 1, place)
        send = lax.dynamic_slice_in_dim(values, 1 - mine, 1, place)
        values = keep + exchange(send, axis, bit)
    return values.reshape(values.shape[len(steps) :])


def ordered_gather(values, steps, order):
    values = values.reshape((1,) * len(steps) + values.shape)
    for axis, bit in reversed(order):
        place = steps.index((axis, bit))
        mine = (lax.axis_index(axis) >> bit) & 1
        other = exchange(values, axis, bit)
        values = jnp.where(
            mine == 0,
            jnp.concatenate([values, other], axis=place),
            jnp.concatenate([other, values], axis=place),
        )
    return values.reshape((-1,) + values.shape[len(steps) + 1 :])


def exchange(values, axis, bit):
    count = lax.axis_size(axis)
    return lax.ppermute(values, axis, [(source, source ^ (1 << bit)) for source in range(count)])


def halving_scatter(values, steps):
    for axis, bit in steps:
        mine = (lax.axis_index(axis) >> bit) & 1
        half = values.shape[0] // 2
        keep = lax.dynamic_slice_in_dim(values, mine * half, half, 0)
        send = lax.dynamic_slice_in_dim(values, (1 - mine) * half, half, 0)
        values = keep + exchange(send, axis, bit)
    return values


def exchange_sum(values, steps):
    for axis, bit in steps:
        values = values + exchange(values, axis, bit)
    return values


def doubling_gather(values, steps):
    for axis, bit in reversed(steps):
        mine = (lax.axis_index(axis) >> bit) & 1
        other = exchange(values, axis, bit)
        values = jnp.where(
            mine == 0,
            jnp.concatenate([values, other], axis=0),
            jnp.concatenate([other, values], axis=0),
        )
    return values


def stacked_tables(dft_real, dft_imag):
    rows = lambda top, bottom: jnp.concatenate([top, bottom], axis=0)
    cols = lambda left, right: jnp.concatenate([left, right], axis=1)
    return (
        rows(dft_real, dft_imag),
        rows(-dft_imag, dft_real),
        cols(dft_real, dft_imag),
        cols(-dft_imag, dft_real),
        rows(dft_real, -dft_imag),
        rows(dft_imag, dft_real),
        cols(dft_real, -dft_imag),
        cols(dft_imag, dft_real),
    )


def patch_kernel(meta_ref, window_ref, amp_ref, probe_ref, *refs):
    tables = refs[:8]
    grad_ref, probe_sum_ref, energy_ref = refs[8:]
    slot = pl.program_id(0)
    slots = pl.num_programs(0)
    side = probe_ref.shape[1]

    @pl.when(slot == 0)
    def _():
        grad_ref[...] = jnp.zeros(grad_ref.shape, jnp.float32)
        probe_sum_ref[...] = jnp.zeros(probe_sum_ref.shape, jnp.float32)
        energy_ref[...] = jnp.zeros(energy_ref.shape, jnp.float32)

    @pl.when(slot < meta_ref[0])
    def _():
        row = meta_ref[1 + slot]
        col = meta_ref[1 + slots + slot]
        band = side + 8
        rows = pl.ds(pl.multiple_of(row // 8 * 8, 8), band)
        row_shift = row % 8
        span = side + 128
        cols = pl.ds(pl.multiple_of(col // 128 * 128, 128), span)
        col_shift = col % 128
        to_front = (span - col_shift) % span

        def extract(part):
            values = pltpu.roll(window_ref[part, rows, cols], (band - row_shift) % band, 0)
            return pltpu.roll(values[:side], to_front, 1)[:, :side]

        patch_real = extract(0)
        patch_imag = extract(1)
        dot = lambda left, right: jnp.dot(left, right, preferred_element_type=jnp.float32)
        left_1a, left_1b, right_2a, right_2b, left_3a, left_3b, right_4a, right_4b = (
            table[...] for table in tables
        )
        probe_real = probe_ref[0]
        probe_imag = probe_ref[1]
        wave_real = (probe_real * patch_real - probe_imag * patch_imag).astype(jnp.bfloat16)
        wave_imag = (probe_real * patch_imag + probe_imag * patch_real).astype(jnp.bfloat16)
        half = (dot(left_1a, wave_real) + dot(left_1b, wave_imag)).astype(jnp.bfloat16)
        far = dot(half[:side], right_2a) + dot(half[side:], right_2b)
        far_real = far[:, :side]
        far_imag = far[:, side:]
        modulus = jnp.sqrt(far_real * far_real + far_imag * far_imag + 0.25)
        factor = amp_ref[0].astype(jnp.float32) / modulus - 1.0
        diff_real = (far_real * factor).astype(jnp.bfloat16)
        diff_imag = (far_imag * factor).astype(jnp.bfloat16)
        back_half = (dot(left_3a, diff_real) + dot(left_3b, diff_imag)).astype(jnp.bfloat16)
        back = dot(back_half[:side], right_4a) + dot(back_half[side:], right_4b)
        back_real = back[:, :side]
        back_imag = back[:, side:]
        filler = jnp.zeros((side, span - side), jnp.float32)
        below = jnp.zeros((8, span), jnp.float32)
        for part, value in enumerate(
            (
                probe_real * back_real + probe_imag * back_imag,
                probe_real * back_imag - probe_imag * back_real,
            )
        ):
            placed = pltpu.roll(jnp.concatenate([value, filler], axis=1), col_shift, 1)
            placed = pltpu.roll(jnp.concatenate([placed, below], axis=0), row_shift, 0)
            grad_ref[part, rows, cols] += placed
        probe_sum_ref[0] += patch_real * back_real + patch_imag * back_imag
        probe_sum_ref[1] += patch_real * back_imag - patch_imag * back_real
        energy = jnp.sum(patch_real * patch_real + patch_imag * patch_imag) / (side * side)
        energy_ref[...] += energy


def patch_terms_all(meta, window, amps, probe_field, tables):
    slots, side, _ = amps.shape
    full = lambda shape: pl.BlockSpec(shape, lambda slot, meta_ref: (0,) * len(shape))
    grid_spec = pltpu.PrefetchScalarGridSpec(
        num_scalar_prefetch=1,
        grid=(slots,),
        in_specs=[
            full(window.shape),
            pl.BlockSpec((1, side, side), lambda slot, meta_ref: (slot, 0, 0)),
            full((2, side, side)),
        ]
        + [full(table.shape) for table in tables],
        out_specs=[
            full(window.shape),
            full((2, side, side)),
            full((8, 128)),
        ],
    )
    return pl.pallas_call(
        patch_kernel,
        grid_spec=grid_spec,
        out_shape=[
            jax.ShapeDtypeStruct(window.shape, jnp.float32),
            jax.ShapeDtypeStruct((2, side, side), jnp.float32),
            jax.ShapeDtypeStruct((8, 128), jnp.float32),
        ],
        compiler_params=pltpu.CompilerParams(dimension_semantics=("arbitrary",)),
    )(meta, window, amps, probe_field, *tables)


def tile_edges(values, offset):
    return shifted(values, "tile", offset)


def on_device(
    object_field,
    probe_field,
    amplitudes,
    pos_rows,
    pos_cols,
    counts,
    admm_dual,
    volume,
    proj_weights,
    ray_weights,
    angle_ids,
):
    half_side = PB // 2
    own_object = object_field[0]
    tile_cols = own_object.shape[2]
    from_left = tile_edges(own_object[:, :, tile_cols - half_side :], 1)
    from_right = tile_edges(own_object[:, :, :half_side], -1)
    extended = jnp.concatenate([from_left, own_object, from_right], axis=2)
    dft_real, dft_imag = dft_tables(PB)
    probe_real = probe_field[0]
    probe_imag = probe_field[1]

    spare = -(-extended.shape[2] // 128) * 128 + 128 - extended.shape[2]
    window = jnp.pad(extended, ((0, 0), (0, 8), (0, spare)))
    meta = jnp.concatenate([counts[0, :1], pos_rows[0, 0], pos_cols[0, 0]])
    grad_sum, probe_sum, energy_rows = patch_terms_all(
        meta,
        window,
        amplitudes[0, 0],
        probe_field,
        stacked_tables(dft_real, dft_imag),
    )
    energy_sum = energy_rows[0, 0]
    grad_sum = grad_sum[:, : extended.shape[1]]
    to_right_edge = tile_edges(grad_sum[:, :, :half_side], -1)
    to_left_edge = tile_edges(grad_sum[:, :, tile_cols + half_side : tile_cols + PB], 1)
    own_cells = grad_sum[:, :, half_side : half_side + tile_cols]
    own_cells = own_cells.at[:, :, :half_side].add(to_left_edge)
    own_cells = own_cells.at[:, :, tile_cols - half_side :].add(to_right_edge)
    probe_order = link_order(bit_steps(("proj", "tile", "cuts")))
    probe_steps, probe_rest = probe_order[:3], probe_order[3:]
    probe_rows = probe_sum.size // 128
    padded_rows = -(-(probe_rows + 1) // 2 ** len(probe_steps)) * 2 ** len(probe_steps)
    probe_flat = jnp.concatenate(
        [
            probe_sum.reshape(probe_rows, 128),
            jnp.broadcast_to(energy_sum, (1, 128)),
            jnp.zeros((padded_rows - probe_rows - 1, 128), jnp.float32),
        ]
    )
    probe_flat = exchange_sum(halving_scatter(probe_flat, probe_steps), probe_rest)
    probe_flat = doubling_gather(probe_flat, probe_steps)
    probe_grad = probe_flat[:probe_rows].reshape(probe_sum.shape)
    energy = probe_flat[probe_rows, 0]
    new_probe = probe_field + probe_grad / (energy + 1e-05)
    probe_peak = jnp.max(probe_real * probe_real + probe_imag * probe_imag)
    new_object = (own_object + own_cells / (probe_peak + 1e-05))[None]
    slab_total = admm_dual.shape[1]
    first_row = (own_object.shape[1] - slab_total) // 2
    slab_values = new_object[:, 1, first_row : first_row + slab_total, :] + admm_dual
    proj_count = lax.axis_size("proj")
    cuts_count = lax.axis_size("cuts")
    slab_dev = slab_total // cuts_count
    u_share = slab_values.shape[2] // proj_count
    projections = proj_count * cuts_count
    pieces = (
        slab_values.reshape(cuts_count, slab_dev, proj_count, u_share)
        .transpose(2, 0, 1, 3)
        .reshape(projections, slab_dev, u_share)
    )
    arrived = lax.all_to_all(pieces, ("proj", "cuts"), 0, 0, tiled=True)
    target = arrived.transpose(2, 0, 1).reshape(u_share, projections * slab_dev)
    angle_count = ray_weights.shape[0]
    x_share = volume.shape[1]
    width = volume.shape[2]
    onehot = (angle_ids[:, None] == jnp.arange(angle_count, dtype=jnp.int32)[None, :]).astype(
        jnp.float32
    )
    ray_table = jnp.dot(
        onehot, ray_weights, precision=lax.Precision.HIGHEST, preferred_element_type=jnp.float32
    )
    ray_sums = jnp.einsum("zxy,ay->azx", volume, ray_table, precision=lax.Precision.HIGHEST).astype(
        jnp.bfloat16
    )
    spread = onehot.astype(jnp.bfloat16)[:, :, None, None] * ray_sums[:, None, :, :]
    spread = spread.transpose(1, 3, 0, 2).reshape(angle_count * x_share, projections * slab_dev)
    weight_flat = proj_weights.reshape(angle_count * x_share, width)
    partial_term = lax.dot_general(
        weight_flat, spread, (((0,), (0,)), ((), ())), preferred_element_type=jnp.float32
    )
    volume_steps = bit_steps(("tile", "proj"))
    volume_order = link_order(volume_steps)
    own_rows = ordered_scatter(partial_term, volume_steps, volume_order)
    own_residue = (own_rows - target).astype(jnp.bfloat16)
    residue = ordered_gather(own_residue, volume_steps, volume_order)
    backproj = matmul(weight_flat, residue)
    backproj = backproj.reshape(angle_count, x_share, projections, slab_dev)
    back_sums = jnp.sum(backproj * onehot.T[:, None, :, None], axis=0).transpose(1, 2, 0)
    gradient = jnp.einsum("azx,ay->zxy", back_sums, ray_table, precision=lax.Precision.HIGHEST)
    new_volume = volume - tomo_step * gradient
    return (new_object, new_probe, new_volume)


def solution(mesh):
    in_specs = (
        P(("proj", "cuts"), None, None, "tile"),
        P(),
        P(("proj", "cuts"), "tile", None, None, None),
        P(("proj", "cuts"), "tile", None),
        P(("proj", "cuts"), "tile", None),
        P(("proj", "cuts"), "tile"),
        P(("proj", "cuts"), None, "tile"),
        P("cuts", ("tile", "proj"), None),
        P(None, ("tile", "proj"), None),
        P(),
        P(),
    )
    out_specs = (P(("proj", "cuts"), None, None, "tile"), P(), P("cuts", ("tile", "proj"), None))
    return jax.shard_map(
        on_device, mesh=mesh, in_specs=in_specs, out_specs=out_specs, check_vma=False
    )
```

```python
import math

import jax
import jax.numpy as jnp
from jax import lax
from jax.experimental import pallas as pl
from jax.experimental.pallas import tpu as pltpu
from jax.sharding import PartitionSpec as P

PB = 256


tomo_step = 1.0


def shifted(value, axis, steps):
    count = lax.axis_size(axis)
    leading, last = (max(0, -steps), min(count, count - steps))
    return lax.ppermute(value, axis, [(source, source + steps) for source in range(leading, last)])


def dft_tables(side):
    indices = jnp.arange(side, dtype=jnp.int32)
    products = indices[:, None] * indices[None, :] % side
    phase_angle = products.astype(jnp.float32) * (2.0 * math.pi / side)
    norm_factor = 1.0 / math.sqrt(side)
    return (
        (jnp.cos(phase_angle) * norm_factor).astype(jnp.bfloat16),
        (-jnp.sin(phase_angle) * norm_factor).astype(jnp.bfloat16),
    )


def matmul(left, right):
    return jnp.dot(left, right, preferred_element_type=jnp.float32)


def complex_matmul(left_real, left_imag, right_real, right_imag):
    out_real = matmul(left_real, right_real) - matmul(left_imag, right_imag)
    out_imag = matmul(left_real, right_imag) + matmul(left_imag, right_real)
    return (out_real, out_imag)


def patch_terms(patch_real, patch_imag, probe_real, probe_imag, amplitude, dft_real, dft_imag):
    wave_real = (probe_real * patch_real - probe_imag * patch_imag).astype(jnp.bfloat16)
    wave_imag = (probe_real * patch_imag + probe_imag * patch_real).astype(jnp.bfloat16)
    half_real, half_imag = complex_matmul(dft_real, dft_imag, wave_real, wave_imag)
    half_real = half_real.astype(jnp.bfloat16)
    half_imag = half_imag.astype(jnp.bfloat16)
    far_real, far_imag = complex_matmul(half_real, half_imag, dft_real, dft_imag)
    modulus = jnp.sqrt(far_real * far_real + far_imag * far_imag + 0.25)
    factor = amplitude.astype(jnp.float32) / modulus - 1.0
    diff_real = (far_real * factor).astype(jnp.bfloat16)
    diff_imag = (far_imag * factor).astype(jnp.bfloat16)
    conj_imag = -dft_imag
    back_half_real, back_half_imag = complex_matmul(dft_real, conj_imag, diff_real, diff_imag)
    back_half_real = back_half_real.astype(jnp.bfloat16)
    back_half_imag = back_half_imag.astype(jnp.bfloat16)
    back_real, back_imag = complex_matmul(back_half_real, back_half_imag, dft_real, conj_imag)
    object_real = probe_real * back_real + probe_imag * back_imag
    object_imag = probe_real * back_imag - probe_imag * back_real
    probe_grad_real = patch_real * back_real + patch_imag * back_imag
    probe_grad_imag = patch_real * back_imag - patch_imag * back_real
    energy = jnp.mean(patch_real * patch_real + patch_imag * patch_imag)
    return (
        jnp.stack([object_real, object_imag]),
        jnp.stack([probe_grad_real, probe_grad_imag]),
        energy,
    )


def axis_bits(axis):
    return lax.axis_size(axis).bit_length() - 1


def bit_steps(axes):
    steps = []
    for axis in axes:
        steps += [(axis, bit) for bit in reversed(range(axis_bits(axis)))]
    return steps


def link_order(steps):
    by_distance = [("proj", 0), ("tile", 0), ("cuts", 0), ("proj", 2), ("tile", 1), ("cuts", 1)]
    ranked = [step for step in by_distance if step in steps]
    return ranked + [step for step in steps if step not in ranked]


def bit_view(values, steps):
    return values.reshape((2,) * len(steps) + (values.shape[0] >> len(steps),) + values.shape[1:])


def ordered_scatter(values, steps, order):
    values = bit_view(values, steps)
    for axis, bit in order:
        place = steps.index((axis, bit))
        mine = (lax.axis_index(axis) >> bit) & 1
        keep = lax.dynamic_slice_in_dim(values, mine, 1, place)
        send = lax.dynamic_slice_in_dim(values, 1 - mine, 1, place)
        values = keep + exchange(send, axis, bit)
    return values.reshape(values.shape[len(steps) :])


def ordered_gather(values, steps, order):
    values = values.reshape((1,) * len(steps) + values.shape)
    for axis, bit in reversed(order):
        place = steps.index((axis, bit))
        mine = (lax.axis_index(axis) >> bit) & 1
        other = exchange(values, axis, bit)
        values = jnp.where(
            mine == 0,
            jnp.concatenate([values, other], axis=place),
            jnp.concatenate([other, values], axis=place),
        )
    return values.reshape((-1,) + values.shape[len(steps) + 1 :])


def exchange(values, axis, bit):
    count = lax.axis_size(axis)
    return lax.ppermute(values, axis, [(source, source ^ (1 << bit)) for source in range(count)])


def halving_scatter(values, steps):
    for axis, bit in steps:
        mine = (lax.axis_index(axis) >> bit) & 1
        half = values.shape[0] // 2
        keep = lax.dynamic_slice_in_dim(values, mine * half, half, 0)
        send = lax.dynamic_slice_in_dim(values, (1 - mine) * half, half, 0)
        values = keep + exchange(send, axis, bit)
    return values


def exchange_sum(values, steps):
    for axis, bit in steps:
        values = values + exchange(values, axis, bit)
    return values


def doubling_gather(values, steps):
    for axis, bit in reversed(steps):
        mine = (lax.axis_index(axis) >> bit) & 1
        other = exchange(values, axis, bit)
        values = jnp.where(
            mine == 0,
            jnp.concatenate([values, other], axis=0),
            jnp.concatenate([other, values], axis=0),
        )
    return values


def stacked_tables(dft_real, dft_imag):
    rows = lambda top, bottom: jnp.concatenate([top, bottom], axis=0)
    cols = lambda left, right: jnp.concatenate([left, right], axis=1)
    return (
        rows(dft_real, dft_imag),
        rows(-dft_imag, dft_real),
        cols(dft_real, dft_imag),
        cols(-dft_imag, dft_real),
        rows(dft_real, -dft_imag),
        rows(dft_imag, dft_real),
        cols(dft_real, -dft_imag),
        cols(dft_imag, dft_real),
    )


def patch_kernel(meta_ref, window_ref, amp_ref, probe_ref, *refs):
    tables = refs[:8]
    grad_ref, probe_sum_ref, energy_ref = refs[8:]
    slot = pl.program_id(0)
    slots = pl.num_programs(0)
    side = probe_ref.shape[1]

    @pl.when(slot == 0)
    def _():
        grad_ref[...] = jnp.zeros(grad_ref.shape, jnp.float32)
        probe_sum_ref[...] = jnp.zeros(probe_sum_ref.shape, jnp.float32)
        energy_ref[...] = jnp.zeros(energy_ref.shape, jnp.float32)

    @pl.when(slot < meta_ref[0])
    def _():
        row = meta_ref[1 + slot]
        col = meta_ref[1 + slots + slot]
        band = side + 8
        rows = pl.ds(pl.multiple_of(row // 8 * 8, 8), band)
        row_shift = row % 8
        span = side + 128
        cols = pl.ds(pl.multiple_of(col // 128 * 128, 128), span)
        col_shift = col % 128
        to_front = (span - col_shift) % span

        def extract(part):
            values = pltpu.roll(window_ref[part, rows, cols], (band - row_shift) % band, 0)
            return pltpu.roll(values[:side], to_front, 1)[:, :side]

        patch_real = extract(0)
        patch_imag = extract(1)
        dot = lambda left, right: jnp.dot(left, right, preferred_element_type=jnp.float32)
        left_1a, left_1b, right_2a, right_2b, left_3a, left_3b, right_4a, right_4b = (
            table[...] for table in tables
        )
        probe_real = probe_ref[0]
        probe_imag = probe_ref[1]
        wave_real = (probe_real * patch_real - probe_imag * patch_imag).astype(jnp.bfloat16)
        wave_imag = (probe_real * patch_imag + probe_imag * patch_real).astype(jnp.bfloat16)
        half = (dot(left_1a, wave_real) + dot(left_1b, wave_imag)).astype(jnp.bfloat16)
        far = dot(half[:side], right_2a) + dot(half[side:], right_2b)
        far_real = far[:, :side]
        far_imag = far[:, side:]
        modulus = jnp.sqrt(far_real * far_real + far_imag * far_imag + 0.25)
        factor = amp_ref[0].astype(jnp.float32) / modulus - 1.0
        diff_real = (far_real * factor).astype(jnp.bfloat16)
        diff_imag = (far_imag * factor).astype(jnp.bfloat16)
        back_half = (dot(left_3a, diff_real) + dot(left_3b, diff_imag)).astype(jnp.bfloat16)
        back = dot(back_half[:side], right_4a) + dot(back_half[side:], right_4b)
        back_real = back[:, :side]
        back_imag = back[:, side:]
        filler = jnp.zeros((side, span - side), jnp.float32)
        below = jnp.zeros((8, span), jnp.float32)
        for part, value in enumerate(
            (
                probe_real * back_real + probe_imag * back_imag,
                probe_real * back_imag - probe_imag * back_real,
            )
        ):
            placed = pltpu.roll(jnp.concatenate([value, filler], axis=1), col_shift, 1)
            placed = pltpu.roll(jnp.concatenate([placed, below], axis=0), row_shift, 0)
            grad_ref[part, rows, cols] += placed
        probe_sum_ref[0] += patch_real * back_real + patch_imag * back_imag
        probe_sum_ref[1] += patch_real * back_imag - patch_imag * back_real
        energy = jnp.sum(patch_real * patch_real + patch_imag * patch_imag) / (side * side)
        energy_ref[...] += energy


def patch_terms_all(meta, window, amps, probe_field, tables):
    slots, side, _ = amps.shape
    full = lambda shape: pl.BlockSpec(shape, lambda slot, meta_ref: (0,) * len(shape))
    grid_spec = pltpu.PrefetchScalarGridSpec(
        num_scalar_prefetch=1,
        grid=(slots,),
        in_specs=[
            full(window.shape),
            pl.BlockSpec((1, side, side), lambda slot, meta_ref: (slot, 0, 0)),
            full((2, side, side)),
        ]
        + [full(table.shape) for table in tables],
        out_specs=[
            full(window.shape),
            full((2, side, side)),
            full((8, 128)),
        ],
    )
    return pl.pallas_call(
        patch_kernel,
        grid_spec=grid_spec,
        out_shape=[
            jax.ShapeDtypeStruct(window.shape, jnp.float32),
            jax.ShapeDtypeStruct((2, side, side), jnp.float32),
            jax.ShapeDtypeStruct((8, 128), jnp.float32),
        ],
        compiler_params=pltpu.CompilerParams(dimension_semantics=("arbitrary",)),
    )(meta, window, amps, probe_field, *tables)


def tile_edges(values, offset):
    return shifted(values, "tile", offset)


def on_device(
    object_field,
    probe_field,
    amplitudes,
    pos_rows,
    pos_cols,
    counts,
    admm_dual,
    volume,
    proj_weights,
    ray_weights,
    angle_ids,
):
    half_side = PB // 2
    own_object = object_field[0]
    tile_cols = own_object.shape[2]
    from_left = tile_edges(own_object[:, :, tile_cols - half_side :], 1)
    from_right = tile_edges(own_object[:, :, :half_side], -1)
    extended = jnp.concatenate([from_left, own_object, from_right], axis=2)
    dft_real, dft_imag = dft_tables(PB)
    probe_real = probe_field[0]
    probe_imag = probe_field[1]

    spare = -(-extended.shape[2] // 128) * 128 + 128 - extended.shape[2]
    window = jnp.pad(extended, ((0, 0), (0, 8), (0, spare)))
    meta = jnp.concatenate([counts[0, :1], pos_rows[0, 0], pos_cols[0, 0]])
    grad_sum, probe_sum, energy_rows = patch_terms_all(
        meta,
        window,
        amplitudes[0, 0],
        probe_field,
        stacked_tables(dft_real, dft_imag),
    )
    energy_sum = energy_rows[0, 0]
    grad_sum = grad_sum[:, : extended.shape[1]]
    to_right_edge = tile_edges(grad_sum[:, :, :half_side], -1)
    to_left_edge = tile_edges(grad_sum[:, :, tile_cols + half_side : tile_cols + PB], 1)
    own_cells = grad_sum[:, :, half_side : half_side + tile_cols]
    own_cells = own_cells.at[:, :, :half_side].add(to_left_edge)
    own_cells = own_cells.at[:, :, tile_cols - half_side :].add(to_right_edge)
    probe_order = link_order(bit_steps(("proj", "tile", "cuts")))
    probe_steps, probe_rest = probe_order[:3], probe_order[3:]
    probe_rows = probe_sum.size // 128
    padded_rows = -(-(probe_rows + 1) // 2 ** len(probe_steps)) * 2 ** len(probe_steps)
    probe_flat = jnp.concatenate(
        [
            probe_sum.reshape(probe_rows, 128),
            jnp.broadcast_to(energy_sum, (1, 128)),
            jnp.zeros((padded_rows - probe_rows - 1, 128), jnp.float32),
        ]
    )
    probe_flat = exchange_sum(halving_scatter(probe_flat, probe_steps), probe_rest)
    probe_flat = doubling_gather(probe_flat, probe_steps)
    probe_grad = probe_flat[:probe_rows].reshape(probe_sum.shape)
    energy = probe_flat[probe_rows, 0]
    new_probe = probe_field + probe_grad / (energy + 1e-05)
    probe_peak = jnp.max(probe_real * probe_real + probe_imag * probe_imag)
    new_object = (own_object + own_cells / (probe_peak + 1e-05))[None]
    slab_total = admm_dual.shape[1]
    first_row = (own_object.shape[1] - slab_total) // 2
    slab_values = new_object[:, 1, first_row : first_row + slab_total, :] + admm_dual
    proj_count = lax.axis_size("proj")
    cuts_count = lax.axis_size("cuts")
    slab_dev = slab_total // cuts_count
    u_share = slab_values.shape[2] // proj_count
    projections = proj_count * cuts_count
    pieces = (
        slab_values.reshape(cuts_count, slab_dev, proj_count, u_share)
        .transpose(2, 0, 1, 3)
        .reshape(projections, slab_dev, u_share)
    )
    arrived = lax.all_to_all(pieces, ("proj", "cuts"), 0, 0, tiled=True)
    target = arrived.transpose(2, 0, 1).reshape(u_share, projections * slab_dev)
    angle_count = ray_weights.shape[0]
    x_share = volume.shape[1]
    width = volume.shape[2]
    onehot = (angle_ids[:, None] == jnp.arange(angle_count, dtype=jnp.int32)[None, :]).astype(
        jnp.float32
    )
    ray_table = jnp.dot(
        onehot, ray_weights, precision=lax.Precision.HIGHEST, preferred_element_type=jnp.float32
    )
    ray_sums = jnp.einsum("zxy,ay->azx", volume, ray_table, precision=lax.Precision.HIGHEST).astype(
        jnp.bfloat16
    )
    spread = onehot.astype(jnp.bfloat16)[:, :, None, None] * ray_sums[:, None, :, :]
    spread = spread.transpose(1, 3, 0, 2).reshape(angle_count * x_share, projections * slab_dev)
    weight_flat = proj_weights.reshape(angle_count * x_share, width)
    partial_term = lax.dot_general(
        weight_flat, spread, (((0,), (0,)), ((), ())), preferred_element_type=jnp.float32
    )
    volume_steps = bit_steps(("tile", "proj"))
    volume_order = link_order(volume_steps)
    own_rows = ordered_scatter(partial_term, volume_steps, volume_order)
    own_residue = (own_rows - target).astype(jnp.bfloat16)
    spread_count = lax.axis_size("tile") * lax.axis_size("proj")
    copies = jnp.broadcast_to(own_residue[None], (spread_count,) + own_residue.shape)
    residue = lax.all_to_all(copies, ("tile", "proj"), 0, 0, tiled=True)
    residue = residue.reshape((-1,) + own_residue.shape[1:])
    backproj = matmul(weight_flat, residue)
    backproj = backproj.reshape(angle_count, x_share, projections, slab_dev)
    back_sums = jnp.sum(backproj * onehot.T[:, None, :, None], axis=0).transpose(1, 2, 0)
    gradient = jnp.einsum("azx,ay->zxy", back_sums, ray_table, precision=lax.Precision.HIGHEST)
    new_volume = volume - tomo_step * gradient
    return (new_object, new_probe, new_volume)


def solution(mesh):
    in_specs = (
        P(("proj", "cuts"), None, None, "tile"),
        P(),
        P(("proj", "cuts"), "tile", None, None, None),
        P(("proj", "cuts"), "tile", None),
        P(("proj", "cuts"), "tile", None),
        P(("proj", "cuts"), "tile"),
        P(("proj", "cuts"), None, "tile"),
        P("cuts", ("tile", "proj"), None),
        P(None, ("tile", "proj"), None),
        P(),
        P(),
    )
    out_specs = (P(("proj", "cuts"), None, None, "tile"), P(), P("cuts", ("tile", "proj"), None))
    return jax.shard_map(
        on_device, mesh=mesh, in_specs=in_specs, out_specs=out_specs, check_vma=False
    )
```

```python
import math

import jax
import jax.numpy as jnp
from jax import lax
from jax.experimental import pallas as pl
from jax.experimental.pallas import tpu as pltpu
from jax.sharding import PartitionSpec as P

PB = 256


tomo_step = 1.0


def shifted(value, axis, steps):
    count = lax.axis_size(axis)
    leading, last = (max(0, -steps), min(count, count - steps))
    return lax.ppermute(value, axis, [(source, source + steps) for source in range(leading, last)])


def dft_tables(side):
    indices = jnp.arange(side, dtype=jnp.int32)
    products = indices[:, None] * indices[None, :] % side
    phase_angle = products.astype(jnp.float32) * (2.0 * math.pi / side)
    norm_factor = 1.0 / math.sqrt(side)
    return (
        (jnp.cos(phase_angle) * norm_factor).astype(jnp.bfloat16),
        (-jnp.sin(phase_angle) * norm_factor).astype(jnp.bfloat16),
    )


def matmul(left, right):
    return jnp.dot(left, right, preferred_element_type=jnp.float32)


def complex_matmul(left_real, left_imag, right_real, right_imag):
    out_real = matmul(left_real, right_real) - matmul(left_imag, right_imag)
    out_imag = matmul(left_real, right_imag) + matmul(left_imag, right_real)
    return (out_real, out_imag)


def patch_terms(patch_real, patch_imag, probe_real, probe_imag, amplitude, dft_real, dft_imag):
    wave_real = (probe_real * patch_real - probe_imag * patch_imag).astype(jnp.bfloat16)
    wave_imag = (probe_real * patch_imag + probe_imag * patch_real).astype(jnp.bfloat16)
    half_real, half_imag = complex_matmul(dft_real, dft_imag, wave_real, wave_imag)
    half_real = half_real.astype(jnp.bfloat16)
    half_imag = half_imag.astype(jnp.bfloat16)
    far_real, far_imag = complex_matmul(half_real, half_imag, dft_real, dft_imag)
    modulus = jnp.sqrt(far_real * far_real + far_imag * far_imag + 0.25)
    factor = amplitude.astype(jnp.float32) / modulus - 1.0
    diff_real = (far_real * factor).astype(jnp.bfloat16)
    diff_imag = (far_imag * factor).astype(jnp.bfloat16)
    conj_imag = -dft_imag
    back_half_real, back_half_imag = complex_matmul(dft_real, conj_imag, diff_real, diff_imag)
    back_half_real = back_half_real.astype(jnp.bfloat16)
    back_half_imag = back_half_imag.astype(jnp.bfloat16)
    back_real, back_imag = complex_matmul(back_half_real, back_half_imag, dft_real, conj_imag)
    object_real = probe_real * back_real + probe_imag * back_imag
    object_imag = probe_real * back_imag - probe_imag * back_real
    probe_grad_real = patch_real * back_real + patch_imag * back_imag
    probe_grad_imag = patch_real * back_imag - patch_imag * back_real
    energy = jnp.mean(patch_real * patch_real + patch_imag * patch_imag)
    return (
        jnp.stack([object_real, object_imag]),
        jnp.stack([probe_grad_real, probe_grad_imag]),
        energy,
    )


def axis_bits(axis):
    return lax.axis_size(axis).bit_length() - 1


def bit_steps(axes):
    steps = []
    for axis in axes:
        steps += [(axis, bit) for bit in reversed(range(axis_bits(axis)))]
    return steps


def link_order(steps):
    by_distance = [("proj", 0), ("tile", 0), ("cuts", 0), ("proj", 2), ("tile", 1), ("cuts", 1)]
    ranked = [step for step in by_distance if step in steps]
    return ranked + [step for step in steps if step not in ranked]


def bit_view(values, steps):
    return values.reshape((2,) * len(steps) + (values.shape[0] >> len(steps),) + values.shape[1:])


def ordered_scatter(values, steps, order):
    values = bit_view(values, steps)
    for axis, bit in order:
        place = steps.index((axis, bit))
        mine = (lax.axis_index(axis) >> bit) & 1
        keep = lax.dynamic_slice_in_dim(values, mine, 1, place)
        send = lax.dynamic_slice_in_dim(values, 1 - mine, 1, place)
        values = keep + exchange(send, axis, bit)
    return values.reshape(values.shape[len(steps) :])


def ordered_gather(values, steps, order):
    values = values.reshape((1,) * len(steps) + values.shape)
    for axis, bit in reversed(order):
        place = steps.index((axis, bit))
        mine = (lax.axis_index(axis) >> bit) & 1
        other = exchange(values, axis, bit)
        values = jnp.where(
            mine == 0,
            jnp.concatenate([values, other], axis=place),
            jnp.concatenate([other, values], axis=place),
        )
    return values.reshape((-1,) + values.shape[len(steps) + 1 :])


def exchange(values, axis, bit):
    count = lax.axis_size(axis)
    return lax.ppermute(values, axis, [(source, source ^ (1 << bit)) for source in range(count)])


def halving_scatter(values, steps):
    for axis, bit in steps:
        mine = (lax.axis_index(axis) >> bit) & 1
        half = values.shape[0] // 2
        keep = lax.dynamic_slice_in_dim(values, mine * half, half, 0)
        send = lax.dynamic_slice_in_dim(values, (1 - mine) * half, half, 0)
        values = keep + exchange(send, axis, bit)
    return values


def exchange_sum(values, steps):
    for axis, bit in steps:
        values = values + exchange(values, axis, bit)
    return values


def doubling_gather(values, steps):
    for axis, bit in reversed(steps):
        mine = (lax.axis_index(axis) >> bit) & 1
        other = exchange(values, axis, bit)
        values = jnp.where(
            mine == 0,
            jnp.concatenate([values, other], axis=0),
            jnp.concatenate([other, values], axis=0),
        )
    return values


def stacked_tables(dft_real, dft_imag):
    rows = lambda top, bottom: jnp.concatenate([top, bottom], axis=0)
    cols = lambda left, right: jnp.concatenate([left, right], axis=1)
    return (
        rows(dft_real, dft_imag),
        rows(-dft_imag, dft_real),
        cols(dft_real, dft_imag),
        cols(-dft_imag, dft_real),
        rows(dft_real, -dft_imag),
        rows(dft_imag, dft_real),
        cols(dft_real, -dft_imag),
        cols(dft_imag, dft_real),
    )


def patch_kernel(meta_ref, window_ref, amp_ref, probe_ref, *refs):
    tables = refs[:8]
    grad_ref, probe_sum_ref, energy_ref = refs[8:]
    slot = pl.program_id(0)
    slots = pl.num_programs(0)
    side = probe_ref.shape[1]

    @pl.when(slot == 0)
    def _():
        grad_ref[...] = jnp.zeros(grad_ref.shape, jnp.float32)
        probe_sum_ref[...] = jnp.zeros(probe_sum_ref.shape, jnp.float32)
        energy_ref[...] = jnp.zeros(energy_ref.shape, jnp.float32)

    @pl.when(slot < meta_ref[0])
    def _():
        row = meta_ref[1 + slot]
        col = meta_ref[1 + slots + slot]
        band = side + 8
        rows = pl.ds(pl.multiple_of(row // 8 * 8, 8), band)
        row_shift = row % 8
        span = side + 128
        cols = pl.ds(pl.multiple_of(col // 128 * 128, 128), span)
        col_shift = col % 128
        to_front = (span - col_shift) % span

        def extract(part):
            values = pltpu.roll(window_ref[part, rows, cols], (band - row_shift) % band, 0)
            return pltpu.roll(values[:side], to_front, 1)[:, :side]

        patch_real = extract(0)
        patch_imag = extract(1)
        dot = lambda left, right: jnp.dot(left, right, preferred_element_type=jnp.float32)
        left_1a, left_1b, right_2a, right_2b, left_3a, left_3b, right_4a, right_4b = (
            table[...] for table in tables
        )
        probe_real = probe_ref[0]
        probe_imag = probe_ref[1]
        wave_real = (probe_real * patch_real - probe_imag * patch_imag).astype(jnp.bfloat16)
        wave_imag = (probe_real * patch_imag + probe_imag * patch_real).astype(jnp.bfloat16)
        half = (dot(left_1a, wave_real) + dot(left_1b, wave_imag)).astype(jnp.bfloat16)
        far = dot(half[:side], right_2a) + dot(half[side:], right_2b)
        far_real = far[:, :side]
        far_imag = far[:, side:]
        modulus = jnp.sqrt(far_real * far_real + far_imag * far_imag + 0.25)
        factor = amp_ref[0].astype(jnp.float32) / modulus - 1.0
        diff_real = (far_real * factor).astype(jnp.bfloat16)
        diff_imag = (far_imag * factor).astype(jnp.bfloat16)
        back_half = (dot(left_3a, diff_real) + dot(left_3b, diff_imag)).astype(jnp.bfloat16)
        back = dot(back_half[:side], right_4a) + dot(back_half[side:], right_4b)
        back_real = back[:, :side]
        back_imag = back[:, side:]
        filler = jnp.zeros((side, span - side), jnp.float32)
        below = jnp.zeros((8, span), jnp.float32)
        for part, value in enumerate(
            (
                probe_real * back_real + probe_imag * back_imag,
                probe_real * back_imag - probe_imag * back_real,
            )
        ):
            placed = pltpu.roll(jnp.concatenate([value, filler], axis=1), col_shift, 1)
            placed = pltpu.roll(jnp.concatenate([placed, below], axis=0), row_shift, 0)
            grad_ref[part, rows, cols] += placed
        probe_sum_ref[0] += patch_real * back_real + patch_imag * back_imag
        probe_sum_ref[1] += patch_real * back_imag - patch_imag * back_real
        energy = jnp.sum(patch_real * patch_real + patch_imag * patch_imag) / (side * side)
        energy_ref[...] += energy


def patch_terms_all(meta, window, amps, probe_field, tables):
    slots, side, _ = amps.shape
    full = lambda shape: pl.BlockSpec(shape, lambda slot, meta_ref: (0,) * len(shape))
    grid_spec = pltpu.PrefetchScalarGridSpec(
        num_scalar_prefetch=1,
        grid=(slots,),
        in_specs=[
            full(window.shape),
            pl.BlockSpec((1, side, side), lambda slot, meta_ref: (slot, 0, 0)),
            full((2, side, side)),
        ]
        + [full(table.shape) for table in tables],
        out_specs=[
            full(window.shape),
            full((2, side, side)),
            full((8, 128)),
        ],
    )
    return pl.pallas_call(
        patch_kernel,
        grid_spec=grid_spec,
        out_shape=[
            jax.ShapeDtypeStruct(window.shape, jnp.float32),
            jax.ShapeDtypeStruct((2, side, side), jnp.float32),
            jax.ShapeDtypeStruct((8, 128), jnp.float32),
        ],
        compiler_params=pltpu.CompilerParams(dimension_semantics=("arbitrary",)),
    )(meta, window, amps, probe_field, *tables)


def tile_edges(values, offset):
    return shifted(values, "tile", offset)


def on_device(
    object_field,
    probe_field,
    amplitudes,
    pos_rows,
    pos_cols,
    counts,
    admm_dual,
    volume,
    proj_weights,
    ray_weights,
    angle_ids,
):
    half_side = PB // 2
    own_object = object_field[0]
    tile_cols = own_object.shape[2]
    from_left = tile_edges(own_object[:, :, tile_cols - half_side :], 1)
    from_right = tile_edges(own_object[:, :, :half_side], -1)
    extended = jnp.concatenate([from_left, own_object, from_right], axis=2)
    dft_real, dft_imag = dft_tables(PB)
    probe_real = probe_field[0]
    probe_imag = probe_field[1]

    spare = -(-extended.shape[2] // 128) * 128 + 128 - extended.shape[2]
    window = jnp.pad(extended, ((0, 0), (0, 8), (0, spare)))
    meta = jnp.concatenate([counts[0, :1], pos_rows[0, 0], pos_cols[0, 0]])
    grad_sum, probe_sum, energy_rows = patch_terms_all(
        meta,
        window,
        amplitudes[0, 0],
        probe_field,
        stacked_tables(dft_real, dft_imag),
    )
    energy_sum = energy_rows[0, 0]
    grad_sum = grad_sum[:, : extended.shape[1]]
    to_right_edge = tile_edges(grad_sum[:, :, :half_side], -1)
    to_left_edge = tile_edges(grad_sum[:, :, tile_cols + half_side : tile_cols + PB], 1)
    own_cells = grad_sum[:, :, half_side : half_side + tile_cols]
    own_cells = own_cells.at[:, :, :half_side].add(to_left_edge)
    own_cells = own_cells.at[:, :, tile_cols - half_side :].add(to_right_edge)
    probe_order = link_order(bit_steps(("proj", "tile", "cuts")))
    probe_steps, probe_rest = probe_order[:3], probe_order[3:]
    probe_rows = probe_sum.size // 128
    padded_rows = -(-(probe_rows + 1) // 2 ** len(probe_steps)) * 2 ** len(probe_steps)
    probe_flat = jnp.concatenate(
        [
            probe_sum.reshape(probe_rows, 128),
            jnp.broadcast_to(energy_sum, (1, 128)),
            jnp.zeros((padded_rows - probe_rows - 1, 128), jnp.float32),
        ]
    )
    probe_flat = exchange_sum(halving_scatter(probe_flat, probe_steps), probe_rest)
    probe_flat = doubling_gather(probe_flat, probe_steps)
    probe_grad = probe_flat[:probe_rows].reshape(probe_sum.shape)
    energy = probe_flat[probe_rows, 0]
    new_probe = probe_field + probe_grad / (energy + 1e-05)
    probe_peak = jnp.max(probe_real * probe_real + probe_imag * probe_imag)
    new_object = (own_object + own_cells / (probe_peak + 1e-05))[None]
    slab_total = admm_dual.shape[1]
    first_row = (own_object.shape[1] - slab_total) // 2
    slab_values = new_object[:, 1, first_row : first_row + slab_total, :] + admm_dual
    proj_count = lax.axis_size("proj")
    cuts_count = lax.axis_size("cuts")
    slab_dev = slab_total // cuts_count
    u_share = slab_values.shape[2] // proj_count
    projections = proj_count * cuts_count
    pieces = (
        slab_values.reshape(cuts_count, slab_dev, proj_count, u_share)
        .transpose(2, 0, 1, 3)
        .reshape(projections, slab_dev, u_share)
    )
    arrived = lax.all_to_all(pieces, ("proj", "cuts"), 0, 0, tiled=True)
    target = arrived.transpose(2, 0, 1).reshape(u_share, projections * slab_dev)
    angle_count = ray_weights.shape[0]
    x_share = volume.shape[1]
    width = volume.shape[2]
    onehot = (angle_ids[:, None] == jnp.arange(angle_count, dtype=jnp.int32)[None, :]).astype(
        jnp.float32
    )
    ray_table = jnp.take(ray_weights, angle_ids, axis=0)
    ray_sums = jnp.einsum("zxy,ay->azx", volume, ray_table, precision=lax.Precision.HIGHEST).astype(
        jnp.bfloat16
    )
    spread = onehot.astype(jnp.bfloat16)[:, :, None, None] * ray_sums[:, None, :, :]
    spread = spread.transpose(1, 3, 0, 2).reshape(angle_count * x_share, projections * slab_dev)
    weight_flat = proj_weights.reshape(angle_count * x_share, width)
    partial_term = lax.dot_general(
        weight_flat, spread, (((0,), (0,)), ((), ())), preferred_element_type=jnp.float32
    )
    volume_steps = bit_steps(("tile", "proj"))
    volume_order = link_order(volume_steps)
    own_rows = ordered_scatter(partial_term, volume_steps, volume_order)
    own_residue = (own_rows - target).astype(jnp.bfloat16)
    residue = ordered_gather(own_residue, volume_steps, volume_order)
    backproj = matmul(weight_flat, residue)
    backproj = backproj.reshape(angle_count, x_share, projections, slab_dev)
    back_sums = jnp.sum(backproj * onehot.T[:, None, :, None], axis=0).transpose(1, 2, 0)
    gradient = jnp.einsum("azx,ay->zxy", back_sums, ray_table, precision=lax.Precision.HIGHEST)
    new_volume = volume - tomo_step * gradient
    return (new_object, new_probe, new_volume)


def solution(mesh):
    in_specs = (
        P(("proj", "cuts"), None, None, "tile"),
        P(),
        P(("proj", "cuts"), "tile", None, None, None),
        P(("proj", "cuts"), "tile", None),
        P(("proj", "cuts"), "tile", None),
        P(("proj", "cuts"), "tile"),
        P(("proj", "cuts"), None, "tile"),
        P("cuts", ("tile", "proj"), None),
        P(None, ("tile", "proj"), None),
        P(),
        P(),
    )
    out_specs = (P(("proj", "cuts"), None, None, "tile"), P(), P("cuts", ("tile", "proj"), None))
    return jax.shard_map(
        on_device, mesh=mesh, in_specs=in_specs, out_specs=out_specs, check_vma=False
    )
```
